32 devices in a mesh: seq: 8 (over y, x, core), head: 4 (over z).
Axes of the slice: x: 2, y: 2, z: 4, core: 2. Of those that a mesh axis runs over, the one named last changes fastest.
Arguments:
- history: bfloat16 [3072, 1024], P('seq'), may hold values from -40 to 40
- w_query: bfloat16 [1024, 256], P(None, 'head'), may hold values from -0.1875 to 0.1875
- w_key: bfloat16 [1024, 256], P(None, 'head'), may hold values from -0.1875 to 0.1875
- w_value: bfloat16 [1024, 256], P(None, 'head'), may hold values from -0.1875 to 0.1875
- w_out: bfloat16 [256, 1024], P('head'), may hold values from -0.375 to 0.375
- norm_gain: float32 [1024], replicated, may hold values from 0.25 to 1.75
- neg_emb: bfloat16 [8192, 1024], P('head'), may hold values from -2 to 2
- pos_emb: bfloat16 [3072, 1024], P('seq'), may hold values from -0.59765625 to 0.59765625
- neg_ids: int32 [8192], P('head'), may hold values from 0 to 15
- target_ids: int32 [3072], P('seq'), may hold values from 0 to 15
- pad_mask: int32 [3072], P('seq'), may hold values 0 or 1
Outputs:
- user_state: bfloat16 [3072, 1024], P('seq', 'head')
- loss: float32 [3072], P('seq')
The draws below stay inside these ranges and needn't reach their ends.
All inputs are finite; a program needn't handle non-finite values. No bound on the sum of `pad_mask` on one device may be relied on, other than what follows from the above.
Results may differ from the reference program's by a relative error of at most 0.012.
Values may be sent and summed in bfloat16 or wider, within the bound.
No kernel may reach another device: no remote copies, remote signals or barrier semaphores. Data moves between devices by JAX's collectives and lax.ppermute only.
A program may use at most 64 MiB of HBM per device.

```python
import jax
import jax.numpy as jnp
from jax import lax

D = 1024
HD = 64
WIN = 256
ITEMS = 16
S_DEV = 384
H = 4
S = 3072
NEG = 8192


def draw_history(key, part):
    first = jax.random.fold_in(jax.random.fold_in(key, 11), 0)
    base = jax.random.normal(first, (S, D), jnp.float32)
    return jnp.clip(base, -6.0, 6.0).astype(jnp.bfloat16)


def draw_neg_emb(key, part):
    first = jax.random.fold_in(jax.random.fold_in(key, 23), 0)
    base = jax.random.normal(first, (NEG, D), jnp.float32)
    unit = D ** (-0.5)
    return jnp.clip(3.0 * unit * base, -2.0, 2.0).astype(jnp.bfloat16)


def set_ends(drawn, rng, least, largest):
    longest = drawn.shape.index(max(drawn.shape))
    spots = []
    for shift in (0, 1):
        where = [jax.random.randint(jax.random.fold_in(rng, axis), (), 0, length) for axis, length in enumerate(drawn.shape)]
        where[longest] = (where[longest] + shift) % drawn.shape[longest]
        spots.append(tuple(where))
    return drawn.at[spots[0]].set(least).at[spots[1]].set(largest)


def level_of(key, extent, cuts, smallest, top_value):
    def one(position, blocks):
        heights = jax.random.uniform(jax.random.fold_in(jax.random.fold_in(key, 6), position), (blocks,), jnp.float32, smallest / len(cuts), top_value / len(cuts))
        return jnp.repeat(jnp.exp(heights), extent[position] // blocks).reshape((-1,) + (1,) * (len(extent) - position - 1))

    factor_of = one(*cuts[0])
    for cut in cuts[1:]:
        factor_of = factor_of * one(*cut)
    return factor_of


def centred(key, extent, width, reach, pieces=(), kind=jnp.bfloat16):
    gain = level_of(key, extent, pieces, -0.22, 0.18) if pieces else 1.0
    array = jax.random.normal(key, extent, jnp.float32) * width * gain
    return jnp.minimum(jnp.maximum(array, -reach), reach).astype(kind)


def setup_inputs(seed: int = 0) -> dict:
    seeds = jax.random.split(jax.random.key(seed), 12)
    history = draw_history(jax.random.fold_in(seeds[11], 71), 0)
    w_query = centred(seeds[1], (D, H * HD), D ** -0.5, 0.1875, ((1, 4),))
    w_key = centred(seeds[2], (D, H * HD), D ** -0.5, 0.1875, ((1, 4),))
    w_value = centred(seeds[3], (D, H * HD), D ** -0.5, 0.1875, ((1, 4),))
    w_out = centred(seeds[4], (H * HD, D), (H * HD) ** -0.5, 0.375, ((0, 4),))
    norm_gain = jnp.clip(1.0 + 0.15 * jax.random.normal(seeds[5], (D,), jnp.float32), 0.25, 1.75)
    neg_emb = draw_neg_emb(jax.random.fold_in(seeds[11], 71), 0)
    pos_emb = centred(seeds[7], (S, D), 0.1, 0.59765625, ((0, 8),))
    neg_ids = set_ends(jax.random.randint(seeds[8], (NEG,), 0, ITEMS), jax.random.fold_in(seeds[8], 1), 0, ITEMS - 1).astype(jnp.int32)
    target_ids = set_ends(jax.random.randint(seeds[9], (S,), 0, ITEMS), jax.random.fold_in(seeds[9], 1), 0, ITEMS - 1).astype(jnp.int32)
    pad_mask = set_ends((jax.random.randint(seeds[10], (S,), 0, 8) < 7).astype(jnp.int32), jax.random.fold_in(seeds[10], 1), 0, 1)
    return dict(history=history, w_query=w_query, w_key=w_key, w_value=w_value, w_out=w_out, norm_gain=norm_gain, neg_emb=neg_emb, pos_emb=pos_emb, neg_ids=neg_ids, target_ids=target_ids, pad_mask=pad_mask)


def reference(history, w_query, w_key, w_value, w_out, norm_gain, neg_emb, pos_emb, neg_ids, target_ids, pad_mask):
    query = jnp.dot(history, w_query, preferred_element_type=jnp.float32).astype(jnp.bfloat16)
    key = jnp.dot(history, w_key, preferred_element_type=jnp.float32).astype(jnp.bfloat16)
    value = jnp.dot(history, w_value, preferred_element_type=jnp.float32).astype(jnp.bfloat16)
    key_pad = jnp.concatenate([jnp.zeros((WIN, H * HD), jnp.bfloat16), key], 0)
    value_pad = jnp.concatenate([jnp.zeros((WIN, H * HD), jnp.bfloat16), value], 0)
    mask_pad = jnp.concatenate([jnp.zeros((WIN,), jnp.int32), pad_mask], 0)
    scale = HD ** (-0.5)
    rows = lax.broadcasted_iota(jnp.int32, (S_DEV, S_DEV + WIN), 0)
    cols = lax.broadcasted_iota(jnp.int32, (S_DEV, S_DEV + WIN), 1)
    diff = rows + WIN - cols
    out_heads = w_out.reshape(H, HD, D).astype(jnp.float32)

    def attend(block):
        start = (block * S_DEV).astype(jnp.int32)
        qb = lax.dynamic_slice_in_dim(query, start, S_DEV, 0).reshape(S_DEV, H, HD).astype(jnp.float32)
        kb = lax.dynamic_slice_in_dim(key_pad, start, S_DEV + WIN, 0).reshape(S_DEV + WIN, H, HD).astype(jnp.float32)
        vb = lax.dynamic_slice_in_dim(value_pad, start, S_DEV + WIN, 0).reshape(S_DEV + WIN, H, HD).astype(jnp.float32)
        mb = lax.dynamic_slice_in_dim(mask_pad, start, S_DEV + WIN, 0)
        allowed = (diff >= 0) & (diff < WIN) & ((mb[None, :] == 1) | (diff == 0))
        scores = jnp.einsum('qhd,khd->hqk', qb, kb) * scale
        scores = jnp.where(allowed[None], scores, -1e+30)
        top = lax.optimization_barrier(jnp.max(scores, -1, keepdims=True))
        weights = jnp.where(allowed[None], jnp.exp(scores - top), 0.0)
        prob = (weights / lax.optimization_barrier(jnp.sum(weights, -1, keepdims=True))).astype(jnp.bfloat16)
        out = jnp.einsum('hqk,khd->qhd', prob.astype(jnp.float32), vb)
        out = out.astype(jnp.bfloat16).astype(jnp.float32)
        head_part = jnp.einsum('qhd,hde->qhe', out, out_heads).astype(jnp.bfloat16)
        head_part = lax.optimization_barrier(head_part)
        return lax.optimization_barrier(jnp.sum(head_part.astype(jnp.float32), 1))
    attn = lax.map(attend, jnp.arange(S // S_DEV, dtype=jnp.int32)).reshape(S, D)
    mean_sq = lax.optimization_barrier(jnp.mean(attn * attn, 1, keepdims=True))
    user_state = (attn * lax.rsqrt(mean_sq + 1e-05) * norm_gain[None, :]).astype(jnp.bfloat16)

    def score_block(block):
        start = (block * S_DEV).astype(jnp.int32)
        ub = lax.dynamic_slice_in_dim(user_state, start, S_DEV, 0)
        pb = lax.dynamic_slice_in_dim(pos_emb, start, S_DEV, 0)
        tb = lax.dynamic_slice_in_dim(target_ids, start, S_DEV, 0)
        neg_logit = lax.dot_general(ub, neg_emb, (((1,), (1,)), ((), ())), preferred_element_type=jnp.float32)
        pos_logit = lax.optimization_barrier(jnp.sum(ub.astype(jnp.float32) * pb.astype(jnp.float32), 1))
        hit = neg_ids[None, :] == tb[:, None]
        masked = jnp.where(hit, -1e+30, neg_logit)
        top = jnp.maximum(lax.optimization_barrier(jnp.max(masked, 1)), pos_logit)
        total = lax.optimization_barrier(jnp.sum(jnp.where(hit, 0.0, jnp.exp(masked - top[:, None])), 1)) + jnp.exp(pos_logit - top)
        return top + jnp.log(total) - pos_logit
    loss = lax.map(score_block, jnp.arange(S // S_DEV, dtype=jnp.int32)).reshape(S)
    return (user_state, loss)
```

```python
import functools

import jax
import jax.numpy as jnp
from jax import lax
from jax.experimental import pallas as pl
from jax.experimental.pallas import tpu as pltpu
from jax.sharding import PartitionSpec as P

HD = 64
WIN = 256
LANES = 128
FLAG_ROWS = 16
LOW = -1e30
MIB = 1 << 20
F32 = jnp.float32
BF16 = jnp.bfloat16
WHOLE = pl.BlockSpec(memory_space=pltpu.VMEM)
RAW = pl.BlockSpec(memory_space=pl.ANY)


def dot_last(a, b):
    return lax.dot_general(a, b, (((1,), (1,)), ((), ())), preferred_element_type=F32)


def dot_plain(a, b):
    return lax.dot_general(a, b, (((1,), (0,)), ((), ())), preferred_element_type=F32)


def from_behind(shard, axis, by):
    count = lax.axis_size(axis)
    pairs = [(i, i + by) for i in range(count) if 0 <= i + by < count]
    return lax.ppermute(shard, axis, pairs)


def partners(axis):
    count = lax.axis_size(axis)
    if count & (count - 1) == 0:
        return [[(i, i ^ k) for i in range(count)] for k in range(count - 1, 0, -1)]
    return [[(i, (i + k) % count) for i in range(count)] for k in range(count - 1, 0, -1)]


def from_all(shard, axis):
    return [shard] + [lax.ppermute(shard, axis, pairs) for pairs in partners(axis)]


def project_body(hist_hbm, wq_ref, wk_ref, wv_ref, pad_ref, q_ref, own_ref, edge_ref, hist, sems):
    rows, width = hist.shape
    cols = wq_ref.shape[0]
    step = LANES
    copies = []
    for n, start in enumerate(range(0, rows, step)):
        part = pl.ds(start, step)
        copies.append(pltpu.make_async_copy(hist_hbm.at[part], hist.at[part], sems.at[n]))
        copies[-1].start()
    weights = jnp.concatenate([wq_ref[...], wk_ref[...], wv_ref[...]], 0)
    flags = jnp.broadcast_to(pad_ref[...], (FLAG_ROWS, rows)).astype(F32).astype(BF16)
    own_ref[2 * cols :, :] = flags
    edge_ref[2 * cols :, :] = flags[:, rows - WIN :]
    for n, start in enumerate(range(0, rows, step)):
        copies[n].wait()
        out = dot_last(hist[start : start + step, :], weights)
        q_ref[start : start + step, :] = out[:, :cols].astype(BF16)
        kv = out[:, cols:].T.astype(BF16)
        own_ref[: 2 * cols, start : start + step] = kv
        if start >= rows - WIN:
            at = start - (rows - WIN)
            edge_ref[: 2 * cols, at : at + step] = kv


def project(history, w_query, w_key, w_value, pad_mask):
    rows, width = history.shape
    cols = w_query.shape[1]
    tall = 2 * cols + FLAG_ROWS
    return pl.pallas_call(
        project_body,
        name="project",
        out_shape=(
            jax.ShapeDtypeStruct((rows, cols), BF16),
            jax.ShapeDtypeStruct((tall, rows), BF16),
            jax.ShapeDtypeStruct((tall, WIN), BF16),
        ),
        in_specs=[RAW, WHOLE, WHOLE, WHOLE, WHOLE],
        out_specs=(WHOLE, WHOLE, WHOLE),
        scratch_shapes=[
            pltpu.VMEM((rows, width), BF16),
            pltpu.SemaphoreType.DMA((rows // LANES,)),
        ],
        compiler_params=pltpu.CompilerParams(vmem_limit_bytes=8 * MIB),
        cost_estimate=pl.CostEstimate(flops=6 * rows * width * cols, bytes_accessed=2 * rows * width, transcendentals=0),
    )(history, w_query.T, w_key.T, w_value.T, pad_mask[None, :])


def attend_body(q_ref, own_ref, prev_ref, out_ref):
    rows, cols = q_ref.shape
    step = LANES
    span = WIN + step
    at_row = lax.broadcasted_iota(jnp.int32, (step, span), 0)
    at_col = lax.broadcasted_iota(jnp.int32, (step, span), 1)
    near = (at_col > at_row) & (at_col <= at_row + WIN)
    self_pos = at_col == at_row + WIN

    def window(lo, hi, first):
        parts = []
        if first < WIN:
            parts.append(prev_ref[lo:hi, first:WIN])
        last = first + span
        if last > WIN:
            parts.append(own_ref[lo:hi, max(first - WIN, 0) : last - WIN])
        return parts[0] if len(parts) == 1 else jnp.concatenate(parts, 1)

    for start in range(0, rows, step):
        flags = window(2 * cols, 2 * cols + FLAG_ROWS, start).astype(F32)[:1]
        allowed = near & ((flags == 1.0) | self_pos)
        for head in range(cols // HD):
            lo = head * HD
            scores = dot_plain(q_ref[start : start + step, lo : lo + HD], window(lo, lo + HD, start)) * HD**-0.5
            scores = jnp.where(allowed, scores, LOW)
            top = jnp.max(scores, 1, keepdims=True)
            weights = jnp.where(allowed, jnp.exp(scores - top), 0.0)
            prob = (weights / jnp.sum(weights, 1, keepdims=True)).astype(BF16)
            value = window(cols + lo, cols + lo + HD, start)
            out_ref[lo : lo + HD, start : start + step] = dot_last(value, prob).astype(BF16)


def attend(query, own, prev):
    rows, cols = query.shape
    return pl.pallas_call(
        attend_body,
        name="attend",
        out_shape=jax.ShapeDtypeStruct((cols, rows), BF16),
        in_specs=[WHOLE] * 3,
        out_specs=WHOLE,
        compiler_params=pltpu.CompilerParams(vmem_limit_bytes=8 * MIB),
        cost_estimate=pl.CostEstimate(flops=4 * rows * 2 * WIN * cols, bytes_accessed=6 * rows * cols, transcendentals=rows * 2 * WIN),
    )(query, own, prev)


def premix_body(count, neg_ref, *refs):
    w_refs = refs[:count]
    gain_ref, gain_here, pos_ref, ids_ref, mix_ref, turned_ref, id_ref, pos_out, scaled = refs[count:]

    @pl.when(pl.program_id(0) == 0)
    def _():
        gain = gain_ref[...]
        for n in range(count):
            piece = w_refs[n][...].astype(F32)
            tall = piece.shape[0]
            scaled[n * tall : (n + 1) * tall, :] = (piece * gain).astype(BF16)
        whole = jnp.concatenate([ref[...].astype(F32) for ref in w_refs], 0)
        turned_ref[...] = whole.T.astype(BF16)
        for n in range(ids_ref.shape[0]):
            line = jnp.broadcast_to(ids_ref[n : n + 1, :], (LANES, LANES))
            id_ref[n * LANES : (n + 1) * LANES, :] = line.T
        pos_out[...] = (pos_ref[...].astype(F32) * gain_here[...]).T

    mix_ref[...] = dot_last(neg_ref[...], scaled[...]).astype(BF16)


def premix(neg_emb, pieces, gain, gain_here, pos_here, neg_ids):
    negs, width = neg_emb.shape
    count = len(pieces)
    deep = count * pieces[0].shape[0]
    rows, share = pos_here.shape
    block = 512
    const = lambda shape: pl.BlockSpec(shape, lambda i: (0, 0))
    return pl.pallas_call(
        functools.partial(premix_body, count),
        name="premix",
        grid=(negs // block,),
        out_shape=(
            jax.ShapeDtypeStruct((negs, deep), BF16),
            jax.ShapeDtypeStruct((width, deep), BF16),
            jax.ShapeDtypeStruct((negs, LANES), jnp.int32),
            jax.ShapeDtypeStruct((share, rows), F32),
        ),
        in_specs=[pl.BlockSpec((block, width), lambda i: (i, 0))]
        + [const(p.shape) for p in pieces]
        + [const((1, width)), const((1, share)), const((rows, share)), const((negs // LANES, LANES))],
        out_specs=(
            pl.BlockSpec((block, deep), lambda i: (i, 0)),
            const((width, deep)),
            const((negs, LANES)),
            const((share, rows)),
        ),
        scratch_shapes=[pltpu.VMEM((deep, width), BF16)],
        compiler_params=pltpu.CompilerParams(vmem_limit_bytes=28 * MIB),
        cost_estimate=pl.CostEstimate(flops=2 * negs * width * deep, bytes_accessed=2 * negs * width, transcendentals=0),
    )(neg_emb, *pieces, gain[None, :], gain_here[None, :], pos_here, neg_ids.reshape(-1, LANES))


def score_body(count, *refs):
    o_refs = refs[:count]
    mix_ref, turned_ref, id_ref, pos_ref, target_ref, here_ref, stat_ref, user_ref, attn, logits = refs[count:]
    width, rows = attn.shape
    share = user_ref.shape[0]
    negs = mix_ref.shape[0]
    block = 256
    heads = jnp.concatenate([ref[...] for ref in o_refs], 0)
    total = jnp.zeros((8, rows), F32)
    for start in range(0, width, block):
        part = dot_plain(turned_ref[start : start + block, :], heads)
        attn[start : start + block, :] = part
        total += jnp.sum((part * part).reshape(block // 8, 8, rows), 0)
    scale = lax.rsqrt(jnp.sum(total, 0, keepdims=True) / width + 1e-05)
    here = pl.multiple_of(here_ref[0] * share, share)
    user = attn[pl.ds(here, share), :] * scale
    user_ref[...] = user
    pos = jnp.sum(user * pos_ref[...], 0, keepdims=True)
    target = target_ref[...]
    top = jnp.full((8, rows), LOW, F32)
    for start in range(0, negs, block):
        part = dot_plain(mix_ref[start : start + block, :], heads) * scale
        ids = id_ref[start : start + block, :]
        hit = jnp.concatenate([ids] * (rows // LANES), 1) == target
        part = jnp.where(hit, LOW, part)
        logits[start : start + block, :] = part
        top = jnp.maximum(top, jnp.max(part.reshape(block // 8, 8, rows), 0))
    top = jnp.max(top, 0, keepdims=True)
    mass = jnp.zeros((8, rows), F32)
    for start in range(0, negs, block):
        part = jnp.exp(logits[start : start + block, :] - top)
        mass += jnp.sum(part.reshape(block // 8, 8, rows), 0)
    mass = jnp.sum(mass, 0, keepdims=True)
    stat_ref[...] = jnp.concatenate([top, mass, pos, pos], 0)


def score(heads, mix, turned, id_cols, pos_turned, target_ids, here):
    count = len(heads)
    negs, deep = mix.shape
    width = turned.shape[0]
    share, rows = pos_turned.shape
    return pl.pallas_call(
        functools.partial(score_body, count),
        name="score",
        out_shape=(
            jax.ShapeDtypeStruct((4, rows), F32),
            jax.ShapeDtypeStruct((share, rows), F32),
        ),
        in_specs=[WHOLE] * (count + 5) + [pl.BlockSpec(memory_space=pltpu.SMEM)],
        out_specs=(WHOLE, WHOLE),
        scratch_shapes=[pltpu.VMEM((width, rows), F32), pltpu.VMEM((negs, rows), F32)],
        compiler_params=pltpu.CompilerParams(vmem_limit_bytes=28 * MIB),
        cost_estimate=pl.CostEstimate(flops=2 * rows * deep * (negs + width), bytes_accessed=2 * negs * deep, transcendentals=negs * rows),
    )(*heads, mix, turned, id_cols, pos_turned, target_ids[None, :], here)


def finish_body(user_ref, gain_ref, out_ref):
    out_ref[...] = (user_ref[...].T * gain_ref[...]).astype(BF16)


def finish(user, gain_here):
    share, rows = user.shape
    return pl.pallas_call(
        finish_body,
        name="finish",
        out_shape=jax.ShapeDtypeStruct((rows, share), BF16),
        in_specs=[WHOLE, WHOLE],
        out_specs=WHOLE,
        compiler_params=pltpu.CompilerParams(vmem_limit_bytes=8 * MIB),
        cost_estimate=pl.CostEstimate(flops=2 * rows * share, bytes_accessed=6 * rows * share, transcendentals=0),
    )(user, gain_here[None, :])


def on_device(
    history,
    w_query,
    w_key,
    w_value,
    w_out,
    norm_gain,
    neg_emb,
    pos_emb,
    neg_ids,
    target_ids,
    pad_mask,
):
    width = history.shape[1]
    share = width // lax.axis_size("head")
    me = lax.axis_index("head")
    pos_here = lax.dynamic_slice_in_dim(pos_emb, me * share, share, 1)
    gain_here = lax.dynamic_slice_in_dim(norm_gain, me * share, share, 0)
    pieces = from_all(w_out, "head")
    query, own, edge = project(history, w_query, w_key, w_value, pad_mask)
    prev = from_behind(edge, "seq", 1)
    heads = from_all(attend(query, own, prev), "head")
    mix, turned, id_cols, pos_turned = premix(neg_emb, pieces, norm_gain, gain_here, pos_here, neg_ids)
    stats, user = score(heads, mix, turned, id_cols, pos_turned, target_ids, me[None].astype(jnp.int32))
    all_stats = from_all(stats, "head")
    user_share = finish(user, gain_here)
    pos_logit = functools.reduce(jnp.add, [s[2] for s in all_stats])
    upper = functools.reduce(jnp.maximum, [s[0] for s in all_stats], pos_logit)
    total = functools.reduce(jnp.add, [s[1] * jnp.exp(s[0] - upper) for s in all_stats])
    loss = upper + jnp.log(total + jnp.exp(pos_logit - upper)) - pos_logit
    return (user_share, loss)


def solution(mesh):
    return jax.shard_map(
        on_device,
        mesh=mesh,
        in_specs=(
            P("seq", None),
            P(None, "head"),
            P(None, "head"),
            P(None, "head"),
            P("head", None),
            P(),
            P("head", None),
            P("seq", None),
            P("head"),
            P("seq"),
            P("seq"),
        ),
        out_specs=(P("seq", "head"), P("seq")),
        check_vma=False,
    )
```

```python
import functools

import jax
import jax.numpy as jnp
from jax import lax
from jax.experimental import pallas as pl
from jax.experimental.pallas import tpu as pltpu
from jax.sharding import PartitionSpec as P


HD = 64
WIN = 256
LANES = 128
FLAG_ROWS = 16
LOW = -1e30
MIB = 1 << 20
F32 = jnp.float32
BF16 = jnp.bfloat16
WHOLE = pl.BlockSpec(memory_space=pltpu.VMEM)
RAW = pl.BlockSpec(memory_space=pltpu.HBM)


def stay(*arrays):
    return [pltpu.with_memory_space_constraint(a, pltpu.HBM) for a in arrays]


def dot_last(a, b):
    return lax.dot_general(a, b, (((1,), (1,)), ((), ())), preferred_element_type=F32)


def dot_plain(a, b):
    return lax.dot_general(a, b, (((1,), (0,)), ((), ())), preferred_element_type=F32)


def from_behind(shard, axis, by):
    count = lax.axis_size(axis)
    pairs = [(i, i + by) for i in range(count) if 0 <= i + by < count]
    return lax.ppermute(shard, axis, pairs)


def partners(axis):
    count = lax.axis_size(axis)
    if count & (count - 1) == 0:
        return [[(i, i ^ k) for i in range(count)] for k in range(1, count)]
    return [[(i, (i + k) % count) for i in range(count)] for k in range(1, count)]


def from_all(shard, axis):
    pieces = [shard]
    for pairs in partners(axis):
        pieces.append(lax.ppermute(shard, axis, pairs))
    return pieces


def fetch_in_pairs(shard):
    count, pairs_of = lax.axis_size("head"), lax.axis_size("seq")
    if count & (count - 1) or pairs_of % 2:
        return from_all(shard, "head")[1:]
    far = []
    for odd in range(1, count, 2):
        moves = [(odd, odd + 1)[s % 2] for s in range(pairs_of)]
        route = [
            (s * count + h, s * count + (h ^ k))
            for s, k in enumerate(moves)
            if k < count
            for h in range(count)
        ]
        far.append(lax.ppermute(shard, ("seq", "head"), route))
    return far


def swap_in_pairs(far, count):
    pairs_of = lax.axis_size("seq")
    if count & (count - 1) or pairs_of % 2:
        return []
    near = []
    for n, piece in enumerate(far):
        both = 2 * n + 2 < count
        route = [(s, s ^ 1) for s in range(pairs_of) if both or s % 2 == 0]
        near.append(lax.ppermute(piece, "seq", route))
    return near


def project_body(hist_hbm, wq_hbm, wk_hbm, wv_hbm, pad_hbm, q_ref, own_ref, edge_ref, hist, weights, pad_ref, sems):
    rows, _ = hist.shape
    cols = wq_hbm.shape[0]
    step = LANES
    starts = list(range(0, rows, step))[::-1]
    copies = []
    for n, source in enumerate((wq_hbm, wk_hbm, wv_hbm)):
        copies.append(pltpu.make_async_copy(source, weights.at[pl.ds(n * cols, cols)], sems.at[n]))
    for n, start in enumerate(starts):
        part = pl.ds(start, step)
        copies.append(pltpu.make_async_copy(hist_hbm.at[part], hist.at[part], sems.at[3 + n]))
    copies.append(pltpu.make_async_copy(pad_hbm, pad_ref, sems.at[3 + len(starts)]))
    for copy in copies:
        copy.start()
    copies[-1].wait()
    pad = jnp.concatenate([pad_ref[n : n + 1, :] for n in range(rows // LANES)], 1)
    flags = jnp.broadcast_to(pad, (FLAG_ROWS, rows)).astype(F32).astype(BF16)
    own_ref[2 * cols :, :] = flags
    edge_ref[2 * cols :, :] = flags[:, rows - WIN :]
    for copy in copies[:3]:
        copy.wait()
    for n, start in enumerate(starts):
        copies[3 + n].wait()
        out = dot_last(hist[start : start + step, :], weights[...])
        q_ref[start : start + step, :] = out[:, :cols].astype(BF16)
        kv = out[:, cols:].T.astype(BF16)
        own_ref[: 2 * cols, start : start + step] = kv
        if start >= rows - WIN:
            at = start - (rows - WIN)
            edge_ref[: 2 * cols, at : at + step] = kv


def project(history, w_query, w_key, w_value, pad_mask):
    rows, width = history.shape
    cols = w_query.shape[1]
    tall = 2 * cols + FLAG_ROWS
    return pl.pallas_call(
        project_body,
        name="project",
        out_shape=(
            jax.ShapeDtypeStruct((rows, cols), BF16),
            jax.ShapeDtypeStruct((tall, rows), BF16),
            jax.ShapeDtypeStruct((tall, WIN), BF16),
        ),
        in_specs=[RAW] * 5,
        out_specs=(WHOLE, WHOLE, WHOLE),
        scratch_shapes=[
            pltpu.VMEM((rows, width), BF16),
            pltpu.VMEM((3 * cols, width), BF16),
            pltpu.VMEM((rows // LANES, LANES), jnp.int32),
            pltpu.SemaphoreType.DMA((4 + rows // LANES,)),
        ],
        compiler_params=pltpu.CompilerParams(vmem_limit_bytes=8 * MIB),
        cost_estimate=pl.CostEstimate(flops=6 * rows * width * cols, bytes_accessed=2 * rows * width, transcendentals=0),
    )(*stay(history, w_query.T, w_key.T, w_value.T, pad_mask.reshape(-1, LANES)))


def attend_body(q_ref, own_ref, prev_ref, out_ref):
    rows, cols = q_ref.shape
    step = LANES
    span = WIN + step
    at_row = lax.broadcasted_iota(jnp.int32, (step, span), 0)
    at_col = lax.broadcasted_iota(jnp.int32, (step, span), 1)
    near = (at_col > at_row) & (at_col <= at_row + WIN)
    self_pos = at_col == at_row + WIN

    def window(lo, hi, first):
        parts = []
        if first < WIN:
            parts.append(prev_ref[lo:hi, first:WIN])
        last = first + span
        if last > WIN:
            parts.append(own_ref[lo:hi, max(first - WIN, 0) : last - WIN])
        return parts[0] if len(parts) == 1 else jnp.concatenate(parts, 1)

    for start in range(0, rows, step):
        flags = window(2 * cols, 2 * cols + FLAG_ROWS, start).astype(F32)[:1]
        allowed = near & ((flags == 1.0) | self_pos)
        for head in range(cols // HD):
            lo = head * HD
            scores = dot_plain(q_ref[start : start + step, lo : lo + HD], window(lo, lo + HD, start)) * HD**-0.5
            scores = jnp.where(allowed, scores, LOW)
            top = jnp.max(scores, 1, keepdims=True)
            weights = jnp.where(allowed, jnp.exp(scores - top), 0.0)
            prob = (weights / jnp.sum(weights, 1, keepdims=True)).astype(BF16)
            value = window(cols + lo, cols + lo + HD, start)
            out_ref[lo : lo + HD, start : start + step] = dot_last(value, prob).astype(BF16)


def attend(query, own, prev):
    rows, cols = query.shape
    return pl.pallas_call(
        attend_body,
        name="attend",
        out_shape=jax.ShapeDtypeStruct((cols, rows), BF16),
        in_specs=[WHOLE] * 3,
        out_specs=WHOLE,
        compiler_params=pltpu.CompilerParams(vmem_limit_bytes=8 * MIB),
        cost_estimate=pl.CostEstimate(flops=4 * rows * 2 * WIN * cols, bytes_accessed=6 * rows * cols, transcendentals=rows * 2 * WIN),
    )(query, own, prev)


def prepare_body(pos_hbm, gain_hbm, ids_hbm, target_hbm, id_ref, pos_out, gain_out, target_out, pos, gain, ids_ref, target_ref, sems):
    rows, share = pos.shape
    here = pl.ds(0, share)
    if pos_hbm.shape[1] != share:
        here = pl.ds(pl.multiple_of(lax.axis_index("head") * share, share), share)
    copy_pos = pltpu.make_async_copy(pos_hbm.at[:, here], pos, sems.at[0])
    copy_gain = pltpu.make_async_copy(gain_hbm.at[:, here], gain, sems.at[1])
    copy_ids = pltpu.make_async_copy(ids_hbm, ids_ref, sems.at[2])
    copy_target = pltpu.make_async_copy(target_hbm, target_ref, sems.at[3])
    copy_ids.start()
    copy_target.start()
    copy_pos.start()
    copy_gain.start()
    copy_ids.wait()
    copy_target.wait()
    target_out[...] = jnp.concatenate([target_ref[n : n + 1, :] for n in range(rows // LANES)], 1)
    for n in range(ids_ref.shape[0]):
        line = jnp.broadcast_to(ids_ref[n : n + 1, :], (LANES, LANES))
        id_ref[n * LANES : (n + 1) * LANES, :] = line.T
    copy_pos.wait()
    copy_gain.wait()
    gain_out[...] = gain[...]
    pos_out[...] = (pos[...].astype(F32) * gain[...]).T


def prepare(pos_emb, norm_gain, neg_ids, target_ids, share):
    rows, _ = pos_emb.shape
    negs = neg_ids.shape[0]
    if share % LANES:
        pos_emb = lax.dynamic_slice_in_dim(pos_emb, lax.axis_index("head") * share, share, 1)
        norm_gain = lax.dynamic_slice_in_dim(norm_gain, lax.axis_index("head") * share, share, 0)
    return pl.pallas_call(
        prepare_body,
        name="prepare",
        out_shape=(
            jax.ShapeDtypeStruct((negs, LANES), jnp.int32),
            jax.ShapeDtypeStruct((share, rows), F32),
            jax.ShapeDtypeStruct((1, share), F32),
            jax.ShapeDtypeStruct((1, rows), jnp.int32),
        ),
        in_specs=[RAW] * 4,
        out_specs=(WHOLE,) * 4,
        scratch_shapes=[
            pltpu.VMEM((rows, share), BF16),
            pltpu.VMEM((1, share), F32),
            pltpu.VMEM((negs // LANES, LANES), jnp.int32),
            pltpu.VMEM((rows // LANES, LANES), jnp.int32),
            pltpu.SemaphoreType.DMA((4,)),
        ],
        compiler_params=pltpu.CompilerParams(vmem_limit_bytes=8 * MIB),
        cost_estimate=pl.CostEstimate(flops=rows * share, bytes_accessed=2 * rows * share, transcendentals=0),
    )(*stay(pos_emb, norm_gain[None, :], neg_ids.reshape(-1, LANES), target_ids.reshape(-1, LANES)))


def premix_body(count, paired, neg_hbm, own_hbm, gain_hbm, *refs):
    n_far = count // 2 if paired else count - 1
    far, near = refs[:n_far], refs[n_far : 2 * n_far if paired else n_far]
    mix_ref, turned_ref, scaled, negs, own, gain, sems = refs[n_far + len(near) :]
    total, _ = negs.shape
    tall = own.shape[0]
    block = 256
    copies = [
        pltpu.make_async_copy(own_hbm, own, sems.at[0]),
        pltpu.make_async_copy(gain_hbm, gain, sems.at[1]),
    ]
    for n, start in enumerate(range(0, total, block)):
        part = pl.ds(start, block)
        copies.append(pltpu.make_async_copy(neg_hbm.at[part], negs.at[part], sems.at[2 + n]))
    for copy in copies:
        copy.start()
    first = lax.axis_index("seq") % 2 == 0
    copies[0].wait()
    copies[1].wait()
    for k in range(count):
        if k == 0:
            piece = own[...].astype(F32)
        elif paired:
            mine, theirs = far[(k - 1) // 2][...].astype(F32), near[(k - 1) // 2][...].astype(F32)
            piece = jnp.where(first, mine, theirs) if k % 2 else jnp.where(first, theirs, mine)
        else:
            piece = far[k - 1][...].astype(F32)
        scaled[k * tall : (k + 1) * tall, :] = (piece * gain[...]).astype(BF16)
        if k % 2:
            pair = jnp.concatenate([last, piece], 0)
            turned_ref[:, (k - 1) * tall : (k + 1) * tall] = pair.T.astype(BF16)
        last = piece
    for n, start in enumerate(range(0, total, block)):
        copies[2 + n].wait()
        mix_ref[start : start + block, :] = dot_last(negs[start : start + block, :], scaled[...]).astype(BF16)


def premix(neg_emb, own, far, near, norm_gain):
    negs, width = neg_emb.shape
    count = lax.axis_size("head")
    tall = own.shape[0]
    deep = count * tall
    return pl.pallas_call(
        functools.partial(premix_body, count, bool(near)),
        name="premix",
        out_shape=(
            jax.ShapeDtypeStruct((negs, deep), BF16),
            jax.ShapeDtypeStruct((width, deep), BF16),
        ),
        in_specs=[RAW, RAW, RAW] + [WHOLE] * (len(far) + len(near)),
        out_specs=(WHOLE, WHOLE),
        scratch_shapes=[
            pltpu.VMEM((deep, width), BF16),
            pltpu.VMEM((negs, width), BF16),
            pltpu.VMEM((tall, width), BF16),
            pltpu.VMEM((1, width), F32),
            pltpu.SemaphoreType.DMA((2 + negs // 256,)),
        ],
        compiler_params=pltpu.CompilerParams(vmem_limit_bytes=28 * MIB),
        cost_estimate=pl.CostEstimate(flops=2 * negs * width * deep, bytes_accessed=2 * negs * width, transcendentals=0),
    )(*stay(neg_emb, own, norm_gain[None, :]), *far, *near)


def score_body(count, *refs):
    o_refs = refs[:count]
    mix_ref, turned_ref, id_ref, pos_ref, target_ref, stat_ref, user_ref, attn, logits = refs[count:]
    width, rows = attn.shape
    share = user_ref.shape[0]
    negs = mix_ref.shape[0]
    block = 256
    heads = jnp.concatenate([ref[...] for ref in o_refs], 0)
    total = jnp.zeros((8, rows), F32)
    for start in range(0, width, block):
        part = dot_plain(turned_ref[start : start + block, :], heads)
        attn[start : start + block, :] = part
        total += jnp.sum((part * part).reshape(block // 8, 8, rows), 0)
    scale = lax.rsqrt(jnp.sum(total, 0, keepdims=True) / width + 1e-05)
    here = pl.multiple_of(lax.axis_index("head") * share, share)
    user = attn[pl.ds(here, share), :] * scale
    user_ref[...] = user
    pos = jnp.sum(user * pos_ref[...], 0, keepdims=True)
    target = target_ref[...]
    top = jnp.full((8, rows), LOW, F32)
    for start in range(0, negs, block):
        part = dot_plain(mix_ref[start : start + block, :], heads) * scale
        ids = id_ref[start : start + block, :]
        hit = jnp.concatenate([ids] * (rows // LANES), 1) == target
        part = jnp.where(hit, LOW, part)
        logits[start : start + block, :] = part
        top = jnp.maximum(top, jnp.max(part.reshape(block // 8, 8, rows), 0))
    top = jnp.max(top, 0, keepdims=True)
    mass = jnp.zeros((8, rows), F32)
    for start in range(0, negs, block):
        part = jnp.exp(logits[start : start + block, :] - top)
        mass += jnp.sum(part.reshape(block // 8, 8, rows), 0)
    mass = jnp.sum(mass, 0, keepdims=True)
    stat_ref[...] = jnp.concatenate([top, mass, pos, pos], 0)


def score(heads, mix, turned, id_cols, pos_turned, target):
    count = len(heads)
    negs, deep = mix.shape
    width = turned.shape[0]
    share, rows = pos_turned.shape
    return pl.pallas_call(
        functools.partial(score_body, count),
        name="score",
        out_shape=(
            jax.ShapeDtypeStruct((4, rows), F32),
            jax.ShapeDtypeStruct((share, rows), F32),
        ),
        in_specs=[WHOLE] * (count + 5),
        out_specs=(WHOLE, WHOLE),
        scratch_shapes=[pltpu.VMEM((width, rows), F32), pltpu.VMEM((negs, rows), F32)],
        compiler_params=pltpu.CompilerParams(vmem_limit_bytes=28 * MIB),
        cost_estimate=pl.CostEstimate(flops=2 * rows * deep * (negs + width), bytes_accessed=2 * negs * deep, transcendentals=negs * rows),
    )(*heads, mix, turned, id_cols, pos_turned, target)


def finish_body(user_ref, gain_ref, out_ref):
    out_ref[...] = (user_ref[...].T * gain_ref[...]).astype(BF16)


def finish(user, gain_here):
    share, rows = user.shape
    return pl.pallas_call(
        finish_body,
        name="finish",
        out_shape=jax.ShapeDtypeStruct((rows, share), BF16),
        in_specs=[WHOLE, WHOLE],
        out_specs=WHOLE,
        compiler_params=pltpu.CompilerParams(vmem_limit_bytes=8 * MIB),
        cost_estimate=pl.CostEstimate(flops=2 * rows * share, bytes_accessed=6 * rows * share, transcendentals=0),
    )(user, gain_here)


def on_device(
    history,
    w_query,
    w_key,
    w_value,
    w_out,
    norm_gain,
    neg_emb,
    pos_emb,
    neg_ids,
    target_ids,
    pad_mask,
):
    width = history.shape[1]
    count = lax.axis_size("head")
    query, own, edge = project(history, w_query, w_key, w_value, pad_mask)
    prev = from_behind(edge, "seq", 1)
    far = fetch_in_pairs(w_out)
    id_cols, pos_turned, gain_here, target = prepare(pos_emb, norm_gain, neg_ids, target_ids, width // count)
    mine = attend(query, own, prev)
    heads = from_all(mine, "head")
    near = swap_in_pairs(far, count)
    mix, turned = premix(neg_emb, w_out, far, near, norm_gain)
    stats, user = score(heads, mix, turned, id_cols, pos_turned, target)
    all_stats = from_all(stats, "head")
    user_share = finish(user, gain_here)
    pos_logit = functools.reduce(jnp.add, [s[2] for s in all_stats])
    upper = functools.reduce(jnp.maximum, [s[0] for s in all_stats], pos_logit)
    total = functools.reduce(jnp.add, [s[1] * jnp.exp(s[0] - upper) for s in all_stats])
    loss = upper + jnp.log(total + jnp.exp(pos_logit - upper)) - pos_logit
    return (user_share, loss)


def solution(mesh):
    return jax.shard_map(
        on_device,
        mesh=mesh,
        in_specs=(
            P("seq", None),
            P(None, "head"),
            P(None, "head"),
            P(None, "head"),
            P("head", None),
            P(),
            P("head", None),
            P("seq", None),
            P("head"),
            P("seq"),
            P("seq"),
        ),
        out_specs=(P("seq", "head"), P("seq")),
        check_vma=False,
    )
```

```python
import functools

import jax
import jax.numpy as jnp
from jax import lax
from jax.experimental import pallas as pl
from jax.experimental.pallas import tpu as pltpu
from jax.sharding import PartitionSpec as P


HD = 64
WIN = 256
LANES = 128
FLAG_ROWS = 16
LOW = -1e30
MIB = 1 << 20
F32 = jnp.float32
BF16 = jnp.bfloat16
WHOLE = pl.BlockSpec(memory_space=pltpu.VMEM)
RAW = pl.BlockSpec(memory_space=pltpu.HBM)


def stay(*arrays):
    return [pltpu.with_memory_space_constraint(a, pltpu.HBM) for a in arrays]


def dot_last(a, b):
    return lax.dot_general(a, b, (((1,), (1,)), ((), ())), preferred_element_type=F32)


def dot_plain(a, b):
    return lax.dot_general(a, b, (((1,), (0,)), ((), ())), preferred_element_type=F32)


def from_behind(shard, axis, by):
    count = lax.axis_size(axis)
    pairs = [(i, i + by) for i in range(count) if 0 <= i + by < count]
    return lax.ppermute(shard, axis, pairs)


def partners(axis):
    count = lax.axis_size(axis)
    if count & (count - 1) == 0:
        return [[(i, i ^ k) for i in range(count)] for k in range(1, count)]
    return [[(i, (i + k) % count) for i in range(count)] for k in range(1, count)]


def from_all(shard, axis):
    pieces = [shard]
    for pairs in partners(axis):
        pieces.append(lax.ppermute(shard, axis, pairs))
    return pieces


def project_body(hist_hbm, wq_hbm, wk_hbm, wv_hbm, pad_hbm, q_ref, own_ref, edge_ref, hist, weights, pad_ref, sems):
    rows, _ = hist.shape
    cols = wq_hbm.shape[0]
    step = LANES
    starts = list(range(0, rows, step))[::-1]
    copies = []
    for n, source in enumerate((wq_hbm, wk_hbm, wv_hbm)):
        copies.append(pltpu.make_async_copy(source, weights.at[pl.ds(n * cols, cols)], sems.at[n]))
    for n, start in enumerate(starts):
        part = pl.ds(start, step)
        copies.append(pltpu.make_async_copy(hist_hbm.at[part], hist.at[part], sems.at[3 + n]))
    copies.append(pltpu.make_async_copy(pad_hbm, pad_ref, sems.at[3 + len(starts)]))
    for copy in copies:
        copy.start()
    copies[-1].wait()
    pad = jnp.concatenate([pad_ref[n : n + 1, :] for n in range(rows // LANES)], 1)
    flags = jnp.broadcast_to(pad, (FLAG_ROWS, rows)).astype(F32).astype(BF16)
    own_ref[2 * cols :, :] = flags
    edge_ref[2 * cols :, :] = flags[:, rows - WIN :]
    for copy in copies[:3]:
        copy.wait()
    for n, start in enumerate(starts):
        copies[3 + n].wait()
        out = dot_last(hist[start : start + step, :], weights[...])
        q_ref[start : start + step, :] = out[:, :cols].astype(BF16)
        kv = out[:, cols:].T.astype(BF16)
        own_ref[: 2 * cols, start : start + step] = kv
        if start >= rows - WIN:
            at = start - (rows - WIN)
            edge_ref[: 2 * cols, at : at + step] = kv


def project(history, w_query, w_key, w_value, pad_mask):
    rows, width = history.shape
    cols = w_query.shape[1]
    tall = 2 * cols + FLAG_ROWS
    return pl.pallas_call(
        project_body,
        name="project",
        out_shape=(
            jax.ShapeDtypeStruct((rows, cols), BF16),
            jax.ShapeDtypeStruct((tall, rows), BF16),
            jax.ShapeDtypeStruct((tall, WIN), BF16),
        ),
        in_specs=[RAW] * 5,
        out_specs=(WHOLE, WHOLE, WHOLE),
        scratch_shapes=[
            pltpu.VMEM((rows, width), BF16),
            pltpu.VMEM((3 * cols, width), BF16),
            pltpu.VMEM((rows // LANES, LANES), jnp.int32),
            pltpu.SemaphoreType.DMA((4 + rows // LANES,)),
        ],
        compiler_params=pltpu.CompilerParams(vmem_limit_bytes=8 * MIB),
        cost_estimate=pl.CostEstimate(flops=6 * rows * width * cols, bytes_accessed=2 * rows * width, transcendentals=0),
    )(*stay(history, w_query.T, w_key.T, w_value.T, pad_mask.reshape(-1, LANES)))


def attend_body(q_ref, own_ref, prev_ref, out_ref):
    rows, cols = q_ref.shape
    step = LANES
    span = WIN + step
    at_row = lax.broadcasted_iota(jnp.int32, (step, span), 0)
    at_col = lax.broadcasted_iota(jnp.int32, (step, span), 1)
    near = (at_col > at_row) & (at_col <= at_row + WIN)
    self_pos = at_col == at_row + WIN

    def window(lo, hi, first):
        parts = []
        if first < WIN:
            parts.append(prev_ref[lo:hi, first:WIN])
        last = first + span
        if last > WIN:
            parts.append(own_ref[lo:hi, max(first - WIN, 0) : last - WIN])
        return parts[0] if len(parts) == 1 else jnp.concatenate(parts, 1)

    for start in range(0, rows, step):
        flags = window(2 * cols, 2 * cols + FLAG_ROWS, start).astype(F32)[:1]
        allowed = near & ((flags == 1.0) | self_pos)
        for head in range(cols // HD):
            lo = head * HD
            scores = dot_plain(q_ref[start : start + step, lo : lo + HD], window(lo, lo + HD, start)) * HD**-0.5
            scores = jnp.where(allowed, scores, LOW)
            top = jnp.max(scores, 1, keepdims=True)
            weights = jnp.where(allowed, jnp.exp(scores - top), 0.0)
            prob = (weights / jnp.sum(weights, 1, keepdims=True)).astype(BF16)
            value = window(cols + lo, cols + lo + HD, start)
            out_ref[lo : lo + HD, start : start + step] = dot_last(value, prob).astype(BF16)


def attend(query, own, prev):
    rows, cols = query.shape
    return pl.pallas_call(
        attend_body,
        name="attend",
        out_shape=jax.ShapeDtypeStruct((cols, rows), BF16),
        in_specs=[WHOLE] * 3,
        out_specs=WHOLE,
        compiler_params=pltpu.CompilerParams(vmem_limit_bytes=8 * MIB),
        cost_estimate=pl.CostEstimate(flops=4 * rows * 2 * WIN * cols, bytes_accessed=6 * rows * cols, transcendentals=rows * 2 * WIN),
    )(query, own, prev)


def prepare_body(pos_hbm, gain_hbm, ids_hbm, target_hbm, own_hbm, neg_hbm, id_ref, pos_out, gain_out, target_out, own_out, all_out, neg_out, pos, ids_ref, target_ref, sems):
    rows, share = pos.shape
    here = pl.ds(0, share)
    if pos_hbm.shape[1] != share:
        here = pl.ds(pl.multiple_of(lax.axis_index("head") * share, share), share)
    moves = (
        (ids_hbm, ids_ref),
        (target_hbm, target_ref),
        (gain_hbm, all_out),
        (pos_hbm.at[:, here], pos),
        (own_hbm, own_out),
        (neg_hbm.at[pl.ds(0, neg_out.shape[0])], neg_out),
    )
    copies = [pltpu.make_async_copy(a, b, sems.at[n]) for n, (a, b) in enumerate(moves)]
    for copy in copies:
        copy.start()
    copies[0].wait()
    copies[1].wait()
    target_out[...] = jnp.concatenate([target_ref[n : n + 1, :] for n in range(rows // LANES)], 1)
    for n in range(ids_ref.shape[0]):
        line = jnp.broadcast_to(ids_ref[n : n + 1, :], (LANES, LANES))
        id_ref[n * LANES : (n + 1) * LANES, :] = line.T
    copies[2].wait()
    copies[3].wait()
    gain = all_out[:, here]
    gain_out[...] = gain
    pos_out[...] = (pos[...].astype(F32) * gain).T
    copies[4].wait()
    copies[5].wait()


def prepare(pos_emb, norm_gain, neg_ids, target_ids, own, neg_emb, share):
    rows, width = pos_emb.shape
    negs = neg_ids.shape[0]
    if share % LANES:
        pos_emb = lax.dynamic_slice_in_dim(pos_emb, lax.axis_index("head") * share, share, 1)
    return pl.pallas_call(
        prepare_body,
        name="prepare",
        out_shape=(
            jax.ShapeDtypeStruct((negs, LANES), jnp.int32),
            jax.ShapeDtypeStruct((share, rows), F32),
            jax.ShapeDtypeStruct((1, share), F32),
            jax.ShapeDtypeStruct((1, rows), jnp.int32),
            jax.ShapeDtypeStruct(own.shape, BF16),
            jax.ShapeDtypeStruct((1, width), F32),
            jax.ShapeDtypeStruct((negs // 2, width), BF16),
        ),
        in_specs=[RAW] * 6,
        out_specs=(WHOLE,) * 7,
        scratch_shapes=[
            pltpu.VMEM((rows, share), BF16),
            pltpu.VMEM((negs // LANES, LANES), jnp.int32),
            pltpu.VMEM((rows // LANES, LANES), jnp.int32),
            pltpu.SemaphoreType.DMA((6,)),
        ],
        compiler_params=pltpu.CompilerParams(vmem_limit_bytes=12 * MIB),
        cost_estimate=pl.CostEstimate(flops=rows * share, bytes_accessed=negs * width, transcendentals=0),
    )(*stay(pos_emb, norm_gain[None, :], neg_ids.reshape(-1, LANES), target_ids.reshape(-1, LANES), own, neg_emb))


def premix_body(count, neg_hbm, first_ref, gain_ref, *refs):
    pieces, (mix_ref, turned_ref, scaled, negs, sems) = refs[:count], refs[count:]
    ahead, width = first_ref.shape
    tall = pieces[0].shape[0]
    block = 256
    copies = {}
    for n, start in enumerate(range(0, negs.shape[0], block)):
        copies[ahead + start] = pltpu.make_async_copy(
            neg_hbm.at[pl.ds(ahead + start, block)], negs.at[pl.ds(start, block)], sems.at[n]
        )
    for copy in copies.values():
        copy.start()
    gain = gain_ref[...]
    for k in range(count):
        scaled[k * tall : (k + 1) * tall, :] = (pieces[k][...].astype(F32) * gain).astype(BF16)
    total = ahead + negs.shape[0]
    turn = width // (total // block)
    for n, start in enumerate(range(0, total, block)):
        if start < ahead:
            part = first_ref[start : start + block, :]
        else:
            copies[start].wait()
            part = negs[start - ahead : start - ahead + block, :]
        mix_ref[start : start + block, :] = dot_last(part, scaled[...]).astype(BF16)
        cols = slice(n * turn, (n + 1) * turn)
        whole = jnp.concatenate([ref[:, cols].astype(F32) for ref in pieces], 0)
        turned_ref[cols, :] = whole.T.astype(BF16)


def premix(neg_emb, first, gain_row, pieces):
    negs, width = neg_emb.shape
    count = len(pieces)
    deep = count * pieces[0].shape[0]
    rest = negs - first.shape[0]
    return pl.pallas_call(
        functools.partial(premix_body, count),
        name="premix",
        out_shape=(
            jax.ShapeDtypeStruct((negs, deep), BF16),
            jax.ShapeDtypeStruct((width, deep), BF16),
        ),
        in_specs=[RAW] + [WHOLE] * (2 + count),
        out_specs=(WHOLE, WHOLE),
        scratch_shapes=[
            pltpu.VMEM((deep, width), BF16),
            pltpu.VMEM((rest, width), BF16),
            pltpu.SemaphoreType.DMA((rest // 256,)),
        ],
        compiler_params=pltpu.CompilerParams(vmem_limit_bytes=28 * MIB),
        cost_estimate=pl.CostEstimate(flops=2 * negs * width * deep, bytes_accessed=2 * negs * width, transcendentals=0),
    )(*stay(neg_emb), first, gain_row, *pieces)


def score_body(count, *refs):
    o_refs = refs[:count]
    mix_ref, turned_ref, id_ref, pos_ref, target_ref, stat_ref, user_ref, attn, logits = refs[count:]
    width, rows = attn.shape
    share = user_ref.shape[0]
    negs = mix_ref.shape[0]
    block = 256
    heads = jnp.concatenate([ref[...] for ref in o_refs], 0)
    total = jnp.zeros((8, rows), F32)
    for start in range(0, width, block):
        part = dot_plain(turned_ref[start : start + block, :], heads)
        attn[start : start + block, :] = part
        total += jnp.sum((part * part).reshape(block // 8, 8, rows), 0)
    scale = lax.rsqrt(jnp.sum(total, 0, keepdims=True) / width + 1e-05)
    here = pl.multiple_of(lax.axis_index("head") * share, share)
    user = attn[pl.ds(here, share), :] * scale
    user_ref[...] = user
    pos = jnp.sum(user * pos_ref[...], 0, keepdims=True)
    target = target_ref[...]
    top = jnp.full((8, rows), LOW, F32)
    for start in range(0, negs, block):
        part = dot_plain(mix_ref[start : start + block, :], heads) * scale
        ids = id_ref[start : start + block, :]
        hit = jnp.concatenate([ids] * (rows // LANES), 1) == target
        part = jnp.where(hit, LOW, part)
        logits[start : start + block, :] = part
        top = jnp.maximum(top, jnp.max(part.reshape(block // 8, 8, rows), 0))
    top = jnp.max(top, 0, keepdims=True)
    mass = jnp.zeros((8, rows), F32)
    for start in range(0, negs, block):
        part = jnp.exp(logits[start : start + block, :] - top)
        mass += jnp.sum(part.reshape(block // 8, 8, rows), 0)
    mass = jnp.sum(mass, 0, keepdims=True)
    stat_ref[...] = jnp.concatenate([top, mass, pos, pos], 0)


def score(heads, mix, turned, id_cols, pos_turned, target):
    count = len(heads)
    negs, deep = mix.shape
    width = turned.shape[0]
    share, rows = pos_turned.shape
    return pl.pallas_call(
        functools.partial(score_body, count),
        name="score",
        out_shape=(
            jax.ShapeDtypeStruct((4, rows), F32),
            jax.ShapeDtypeStruct((share, rows), F32),
        ),
        in_specs=[WHOLE] * (count + 5),
        out_specs=(WHOLE, WHOLE),
        scratch_shapes=[pltpu.VMEM((width, rows), F32), pltpu.VMEM((negs, rows), F32)],
        compiler_params=pltpu.CompilerParams(vmem_limit_bytes=28 * MIB),
        cost_estimate=pl.CostEstimate(flops=2 * rows * deep * (negs + width), bytes_accessed=2 * negs * deep, transcendentals=negs * rows),
    )(*heads, mix, turned, id_cols, pos_turned, target)


def finish_body(user_ref, gain_ref, out_ref):
    out_ref[...] = (user_ref[...].T * gain_ref[...]).astype(BF16)


def finish(user, gain_here):
    share, rows = user.shape
    return pl.pallas_call(
        finish_body,
        name="finish",
        out_shape=jax.ShapeDtypeStruct((rows, share), BF16),
        in_specs=[WHOLE, WHOLE],
        out_specs=WHOLE,
        compiler_params=pltpu.CompilerParams(vmem_limit_bytes=8 * MIB),
        cost_estimate=pl.CostEstimate(flops=2 * rows * share, bytes_accessed=6 * rows * share, transcendentals=0),
    )(user, gain_here)


def on_device(
    history,
    w_query,
    w_key,
    w_value,
    w_out,
    norm_gain,
    neg_emb,
    pos_emb,
    neg_ids,
    target_ids,
    pad_mask,
):
    width = history.shape[1]
    count = lax.axis_size("head")
    query, own, edge = project(history, w_query, w_key, w_value, pad_mask)
    prev = from_behind(edge, "seq", 1)
    pieces = from_all(w_out, "head")
    id_cols, pos_turned, gain_here, target, pieces[0], gain_row, first = prepare(
        pos_emb, norm_gain, neg_ids, target_ids, w_out, neg_emb, width // count
    )
    mine = attend(query, own, prev)
    heads = from_all(mine, "head")
    mix, turned = premix(neg_emb, first, gain_row, pieces)
    stats, user = score(heads, mix, turned, id_cols, pos_turned, target)
    all_stats = from_all(stats, "head")
    user_share = finish(user, gain_here)
    pos_logit = functools.reduce(jnp.add, [s[2] for s in all_stats])
    upper = functools.reduce(jnp.maximum, [s[0] for s in all_stats], pos_logit)
    total = functools.reduce(jnp.add, [s[1] * jnp.exp(s[0] - upper) for s in all_stats])
    loss = upper + jnp.log(total + jnp.exp(pos_logit - upper)) - pos_logit
    return (user_share, loss)


def solution(mesh):
    return jax.shard_map(
        on_device,
        mesh=mesh,
        in_specs=(
            P("seq", None),
            P(None, "head"),
            P(None, "head"),
            P(None, "head"),
            P("head", None),
            P(),
            P("head", None),
            P("seq", None),
            P("head"),
            P("seq"),
            P("seq"),
        ),
        out_specs=(P("seq", "head"), P("seq")),
        check_vma=False,
    )
```

```python
import functools

import jax
import jax.numpy as jnp
from jax import lax
from jax.experimental import pallas as pl
from jax.experimental.pallas import tpu as pltpu
from jax.sharding import PartitionSpec as P


HD = 64
WIN = 256
LANES = 128
FLAG_ROWS = 16
LOW = -1e30
MIB = 1 << 20
AHEAD = 4 * 10**9
F32 = jnp.float32
BF16 = jnp.bfloat16
WHOLE = pl.BlockSpec(memory_space=pltpu.VMEM)
RAW = pl.BlockSpec(memory_space=pltpu.HBM)


def stay(*arrays):
    return [pltpu.with_memory_space_constraint(a, pltpu.HBM) for a in arrays]


def dot_last(a, b):
    return lax.dot_general(a, b, (((1,), (1,)), ((), ())), preferred_element_type=F32)


def dot_plain(a, b):
    return lax.dot_general(a, b, (((1,), (0,)), ((), ())), preferred_element_type=F32)


def from_behind(shard, axis, by):
    count = lax.axis_size(axis)
    pairs = [(i, i + by) for i in range(count) if 0 <= i + by < count]
    return lax.ppermute(shard, axis, pairs)


def partners(axis):
    count = lax.axis_size(axis)
    if count & (count - 1) == 0:
        return [[(i, i ^ k) for i in range(count)] for k in range(1, count)]
    return [[(i, (i + k) % count) for i in range(count)] for k in range(1, count)]


def from_all(shard, axis):
    pieces = [shard]
    for pairs in partners(axis):
        pieces.append(lax.ppermute(shard, axis, pairs))
    return pieces


def is_paired(count, slabs):
    return count & (count - 1) == 0 and slabs % 2 == 0


def fetch_in_pairs(shard, half):
    count, slabs = lax.axis_size("head"), lax.axis_size("seq")
    if not is_paired(count, slabs):
        return from_all(shard, "head")[1:]
    far = []
    for odd in range(1, count, 2):
        last = odd + 1 == count
        route = [
            (s * count + h, s * count + (h ^ (odd if last else odd + s % 2)))
            for s in range(slabs)
            for h in range(count)
        ]
        far.append(lax.ppermute(half if last else shard, ("seq", "head"), route))
    return far


def swap_in_pairs(far, count):
    slabs = lax.axis_size("seq")
    if not is_paired(count, slabs):
        return []
    near = []
    for piece in far:
        near.append(lax.ppermute(piece, "seq", [(s, s ^ 1) for s in range(slabs)]))
    return near


def front_body(*refs):
    hist_hbm, wq_hbm, wk_hbm, wv_hbm, pad_hbm, pos_hbm, gain_hbm, ids_hbm, target_hbm, out_hbm = refs[:10]
    q_ref, own_ref, edge_ref, id_ref, pos_out, gain_out, target_out, gain_row, half_ref = refs[10:19]
    hist, weights, pos, pad_ref, ids_ref, target_ref, sems = refs[19:]
    rows, _ = hist.shape
    cols = wq_hbm.shape[0]
    share = pos.shape[1]
    step = LANES
    here = pl.ds(0, share)
    if pos_hbm.shape[1] != share:
        here = pl.ds(pl.multiple_of(lax.axis_index("head") * share, share), share)
    starts = list(range(0, rows, step))[::-1]
    moves = [(ids_hbm, ids_ref), (target_hbm, target_ref), (pad_hbm, pad_ref), (gain_hbm, gain_row)]
    moves.append((pos_hbm.at[:, here], pos))
    half = half_ref.shape[0]
    part = lax.axis_index("seq") % (out_hbm.shape[0] // half)
    moves.append((out_hbm.at[pl.ds(pl.multiple_of(part * half, half), half)], half_ref))
    for n, source in enumerate((wq_hbm, wk_hbm, wv_hbm)):
        moves.append((source, weights.at[pl.ds(n * cols, cols)]))
    for start in starts:
        moves.append((hist_hbm.at[pl.ds(start, step)], hist.at[pl.ds(start, step)]))
    copies = [pltpu.make_async_copy(a, b, sems.at[n]) for n, (a, b) in enumerate(moves)]
    for copy in copies:
        copy.start()
    for copy in copies[:3]:
        copy.wait()
    for n in range(ids_ref.shape[0]):
        line = jnp.broadcast_to(ids_ref[n : n + 1, :], (LANES, LANES))
        id_ref[n * LANES : (n + 1) * LANES, :] = line.T
    target_out[...] = jnp.concatenate([target_ref[n : n + 1, :] for n in range(rows // LANES)], 1)
    pad = jnp.concatenate([pad_ref[n : n + 1, :] for n in range(rows // LANES)], 1)
    flags = jnp.broadcast_to(pad, (FLAG_ROWS, rows)).astype(F32).astype(BF16)
    own_ref[2 * cols :, :] = flags
    edge_ref[2 * cols :, :] = flags[:, rows - WIN :]
    for copy in copies[3:]:
        copy.wait()
    gain_here = gain_row[:, here]
    gain_out[...] = gain_here
    pos_out[...] = (pos[...].astype(F32) * gain_here).T
    for start in starts:
        out = dot_last(hist[start : start + step, :], weights[...])
        q_ref[start : start + step, :] = out[:, :cols].astype(BF16)
        kv = out[:, cols:].T.astype(BF16)
        own_ref[: 2 * cols, start : start + step] = kv
        if start >= rows - WIN:
            at = start - (rows - WIN)
            edge_ref[: 2 * cols, at : at + step] = kv


def front(history, w_query, w_key, w_value, pad_mask, pos_emb, norm_gain, neg_ids, target_ids, w_out, share):
    rows, width = history.shape
    negs = neg_ids.shape[0]
    half = w_out.shape[0] // 2
    cols = w_query.shape[1]
    tall = 2 * cols + FLAG_ROWS
    if share % LANES:
        pos_emb = lax.dynamic_slice_in_dim(pos_emb, lax.axis_index("head") * share, share, 1)
    by_lanes = lambda a: a.reshape(-1, LANES)
    return pl.pallas_call(
        front_body,
        name="front",
        out_shape=(
            jax.ShapeDtypeStruct((rows, cols), BF16),
            jax.ShapeDtypeStruct((tall, rows), BF16),
            jax.ShapeDtypeStruct((tall, WIN), BF16),
            jax.ShapeDtypeStruct((negs, LANES), jnp.int32),
            jax.ShapeDtypeStruct((share, rows), F32),
            jax.ShapeDtypeStruct((1, share), F32),
            jax.ShapeDtypeStruct((1, rows), jnp.int32),
            jax.ShapeDtypeStruct((1, width), F32),
            jax.ShapeDtypeStruct((half, width), BF16),
        ),
        in_specs=[RAW] * 10,
        out_specs=(WHOLE,) * 9,
        scratch_shapes=[
            pltpu.VMEM((rows, width), BF16),
            pltpu.VMEM((3 * cols, width), BF16),
            pltpu.VMEM((rows, share), BF16),
            pltpu.VMEM((rows // LANES, LANES), jnp.int32),
            pltpu.VMEM((negs // LANES, LANES), jnp.int32),
            pltpu.VMEM((rows // LANES, LANES), jnp.int32),
            pltpu.SemaphoreType.DMA((9 + rows // LANES,)),
        ],
        compiler_params=pltpu.CompilerParams(vmem_limit_bytes=12 * MIB),
        cost_estimate=pl.CostEstimate(flops=AHEAD, bytes_accessed=4 * rows * width, transcendentals=0),
    )(
        *stay(history, w_query.T, w_key.T, w_value.T, by_lanes(pad_mask)),
        *stay(pos_emb, norm_gain[None, :], by_lanes(neg_ids), by_lanes(target_ids), w_out),
    )


def attend_body(q_ref, own_ref, prev_ref, out_ref):
    rows, cols = q_ref.shape
    step = LANES
    span = WIN + step
    at_row = lax.broadcasted_iota(jnp.int32, (step, span), 0)
    at_col = lax.broadcasted_iota(jnp.int32, (step, span), 1)
    near = (at_col > at_row) & (at_col <= at_row + WIN)
    self_pos = at_col == at_row + WIN

    def window(lo, hi, first):
        parts = []
        if first < WIN:
            parts.append(prev_ref[lo:hi, first:WIN])
        last = first + span
        if last > WIN:
            parts.append(own_ref[lo:hi, max(first - WIN, 0) : last - WIN])
        return parts[0] if len(parts) == 1 else jnp.concatenate(parts, 1)

    for start in range(0, rows, step):
        flags = window(2 * cols, 2 * cols + FLAG_ROWS, start).astype(F32)[:1]
        allowed = near & ((flags == 1.0) | self_pos)
        for head in range(cols // HD):
            lo = head * HD
            scores = dot_plain(q_ref[start : start + step, lo : lo + HD], window(lo, lo + HD, start)) * HD**-0.5
            scores = jnp.where(allowed, scores, LOW)
            top = jnp.max(scores, 1, keepdims=True)
            weights = jnp.where(allowed, jnp.exp(scores - top), 0.0)
            prob = (weights / jnp.sum(weights, 1, keepdims=True)).astype(BF16)
            value = window(cols + lo, cols + lo + HD, start)
            out_ref[lo : lo + HD, start : start + step] = dot_last(value, prob).astype(BF16)


def attend(query, own, prev):
    rows, cols = query.shape
    return pl.pallas_call(
        attend_body,
        name="attend",
        out_shape=jax.ShapeDtypeStruct((cols, rows), BF16),
        in_specs=[WHOLE] * 3,
        out_specs=WHOLE,
        compiler_params=pltpu.CompilerParams(vmem_limit_bytes=8 * MIB),
        cost_estimate=pl.CostEstimate(flops=AHEAD, bytes_accessed=6 * rows * cols, transcendentals=rows * 2 * WIN),
    )(query, own, prev)


def premix_body(count, split, neg_ref, gain_ref, own_ref, *refs):
    far, near, (mix_ref, turned_ref, scaled, held) = refs[:split[0]], refs[split[0] : sum(split)], refs[sum(split) :]
    total, width = neg_ref.shape
    tall = own_ref.shape[0]
    block = 256
    gain = gain_ref[...]
    first = lax.axis_index("seq") % 2 == 0
    pieces = [own_ref]
    for k in range(1, count):
        if not near:
            pieces.append(far[k - 1])
            continue
        mine, theirs = far[(k - 1) // 2][...], near[(k - 1) // 2][...]
        even, odd = jnp.where(first, mine, theirs), jnp.where(first, theirs, mine)
        held[k - 1] = jnp.concatenate([even, odd], 0) if k == count - 1 else even if k % 2 else odd
        pieces.append(held.at[k - 1])
    for k in range(count):
        scaled[k * tall : (k + 1) * tall, :] = (pieces[k][...].astype(F32) * gain).astype(BF16)
    turn = width // (total // block)
    for n, start in enumerate(range(0, total, block)):
        part = neg_ref[start : start + block, :]
        mix_ref[start : start + block, :] = dot_last(part, scaled[...]).astype(BF16)
        cols = slice(n * turn, (n + 1) * turn)
        whole = jnp.concatenate([ref[:, cols].astype(F32) for ref in pieces], 0)
        turned_ref[cols, :] = whole.T.astype(BF16)


def premix(neg_emb, gain_row, own, far, near):
    negs, width = neg_emb.shape
    count = lax.axis_size("head")
    tall = own.shape[0]
    deep = count * tall
    return pl.pallas_call(
        functools.partial(premix_body, count, (len(far), len(near))),
        name="premix",
        out_shape=(
            jax.ShapeDtypeStruct((negs, deep), BF16),
            jax.ShapeDtypeStruct((width, deep), BF16),
        ),
        in_specs=[WHOLE] * (3 + len(far) + len(near)),
        out_specs=(WHOLE, WHOLE),
        scratch_shapes=[pltpu.VMEM((deep, width), BF16), pltpu.VMEM((count - 1, tall, width), BF16)],
        compiler_params=pltpu.CompilerParams(vmem_limit_bytes=20 * MIB),
        cost_estimate=pl.CostEstimate(flops=2 * negs * width * deep, bytes_accessed=2 * negs * width, transcendentals=0),
    )(neg_emb, gain_row, own, *far, *near)


def score_body(count, *refs):
    o_refs = refs[:count]
    mix_ref, turned_ref, id_ref, pos_ref, target_ref, stat_ref, user_ref, attn, logits = refs[count:]
    width, rows = attn.shape
    share = user_ref.shape[0]
    negs = mix_ref.shape[0]
    block = 256
    heads = jnp.concatenate([ref[...] for ref in o_refs], 0)
    total = jnp.zeros((8, rows), F32)
    for start in range(0, width, block):
        part = dot_plain(turned_ref[start : start + block, :], heads)
        attn[start : start + block, :] = part
        total += jnp.sum((part * part).reshape(block // 8, 8, rows), 0)
    scale = lax.rsqrt(jnp.sum(total, 0, keepdims=True) / width + 1e-05)
    here = pl.multiple_of(lax.axis_index("head") * share, share)
    user = attn[pl.ds(here, share), :] * scale
    user_ref[...] = user
    pos = jnp.sum(user * pos_ref[...], 0, keepdims=True)
    target = target_ref[...]
    top = jnp.full((8, rows), LOW, F32)
    for start in range(0, negs, block):
        part = dot_plain(mix_ref[start : start + block, :], heads) * scale
        ids = id_ref[start : start + block, :]
        hit = jnp.concatenate([ids] * (rows // LANES), 1) == target
        part = jnp.where(hit, LOW, part)
        logits[start : start + block, :] = part
        top = jnp.maximum(top, jnp.max(part.reshape(block // 8, 8, rows), 0))
    top = jnp.max(top, 0, keepdims=True)
    mass = jnp.zeros((8, rows), F32)
    for start in range(0, negs, block):
        part = jnp.exp(logits[start : start + block, :] - top)
        mass += jnp.sum(part.reshape(block // 8, 8, rows), 0)
    mass = jnp.sum(mass, 0, keepdims=True)
    stat_ref[...] = jnp.concatenate([top, mass, pos, pos], 0)


def score(heads, mix, turned, id_cols, pos_turned, target):
    count = len(heads)
    negs, deep = mix.shape
    width = turned.shape[0]
    share, rows = pos_turned.shape
    return pl.pallas_call(
        functools.partial(score_body, count),
        name="score",
        out_shape=(
            jax.ShapeDtypeStruct((4, rows), F32),
            jax.ShapeDtypeStruct((share, rows), F32),
        ),
        in_specs=[WHOLE] * (count + 5),
        out_specs=(WHOLE, WHOLE),
        scratch_shapes=[pltpu.VMEM((width, rows), F32), pltpu.VMEM((negs, rows), F32)],
        compiler_params=pltpu.CompilerParams(vmem_limit_bytes=28 * MIB),
        cost_estimate=pl.CostEstimate(flops=2 * rows * deep * (negs + width), bytes_accessed=2 * negs * deep, transcendentals=negs * rows),
    )(*heads, mix, turned, id_cols, pos_turned, target)


def finish_body(user_ref, gain_ref, out_ref):
    out_ref[...] = (user_ref[...].T * gain_ref[...]).astype(BF16)


def finish(user, gain_here):
    share, rows = user.shape
    return pl.pallas_call(
        finish_body,
        name="finish",
        out_shape=jax.ShapeDtypeStruct((rows, share), BF16),
        in_specs=[WHOLE, WHOLE],
        out_specs=WHOLE,
        compiler_params=pltpu.CompilerParams(vmem_limit_bytes=8 * MIB),
        cost_estimate=pl.CostEstimate(flops=2 * rows * share, bytes_accessed=6 * rows * share, transcendentals=0),
    )(user, gain_here)


def on_device(
    history,
    w_query,
    w_key,
    w_value,
    w_out,
    norm_gain,
    neg_emb,
    pos_emb,
    neg_ids,
    target_ids,
    pad_mask,
):
    width = history.shape[1]
    count = lax.axis_size("head")
    query, own, edge, id_cols, pos_turned, gain_here, target, gain_row, half = front(
        history, w_query, w_key, w_value, pad_mask, pos_emb, norm_gain, neg_ids, target_ids, w_out, width // count
    )
    prev = from_behind(edge, "seq", 1)
    far = fetch_in_pairs(w_out, half)
    mine = attend(query, own, prev)
    heads = from_all(mine, "head")
    near = swap_in_pairs(far, count)
    mix, turned = premix(neg_emb, gain_row, w_out, far, near)
    stats, user = score(heads, mix, turned, id_cols, pos_turned, target)
    all_stats = from_all(stats, "head")
    user_share = finish(user, gain_here)
    pos_logit = functools.reduce(jnp.add, [s[2] for s in all_stats])
    upper = functools.reduce(jnp.maximum, [s[0] for s in all_stats], pos_logit)
    total = functools.reduce(jnp.add, [s[1] * jnp.exp(s[0] - upper) for s in all_stats])
    loss = upper + jnp.log(total + jnp.exp(pos_logit - upper)) - pos_logit
    return (user_share, loss)


def solution(mesh):
    return jax.shard_map(
        on_device,
        mesh=mesh,
        in_specs=(
            P("seq", None),
            P(None, "head"),
            P(None, "head"),
            P(None, "head"),
            P("head", None),
            P(),
            P("head", None),
            P("seq", None),
            P("head"),
            P("seq"),
            P("seq"),
        ),
        out_specs=(P("seq", "head"), P("seq")),
        check_vma=False,
    )
```

```python
import functools

import jax
import jax.numpy as jnp
from jax import lax
from jax.experimental import pallas as pl
from jax.experimental.pallas import tpu as pltpu
from jax.sharding import PartitionSpec as P


HD = 64
WIN = 256
LANES = 128
FLAG_ROWS = 16
LOW = -1e30
MIB = 1 << 20
AHEAD = 4 * 10**9
F32 = jnp.float32
BF16 = jnp.bfloat16
WHOLE = pl.BlockSpec(memory_space=pltpu.VMEM)
RAW = pl.BlockSpec(memory_space=pltpu.HBM)


def stay(*arrays):
    return [pltpu.with_memory_space_constraint(a, pltpu.HBM) for a in arrays]


def dot_last(a, b):
    return lax.dot_general(a, b, (((1,), (1,)), ((), ())), preferred_element_type=F32)


def dot_plain(a, b):
    return lax.dot_general(a, b, (((1,), (0,)), ((), ())), preferred_element_type=F32)


def from_behind(shard, axis, by):
    count = lax.axis_size(axis)
    pairs = [(i, i + by) for i in range(count) if 0 <= i + by < count]
    return lax.ppermute(shard, axis, pairs)


def partners(axis):
    count = lax.axis_size(axis)
    if count & (count - 1) == 0:
        return [[(i, i ^ k) for i in range(count)] for k in range(1, count)]
    return [[(i, (i + k) % count) for i in range(count)] for k in range(1, count)]


def from_all(shard, axis):
    pieces = [shard]
    for pairs in partners(axis):
        pieces.append(lax.ppermute(shard, axis, pairs))
    return pieces


def is_paired(count, slabs):
    return count & (count - 1) == 0 and slabs % 2 == 0


def fetch_in_pairs(shard, half):
    count, slabs = lax.axis_size("head"), lax.axis_size("seq")
    if not is_paired(count, slabs):
        return from_all(shard, "head")[1:]
    far = []
    for odd in range(1, count, 2):
        last = odd + 1 == count
        route = [
            (s * count + h, s * count + (h ^ (odd if last else odd + s % 2)))
            for s in range(slabs)
            for h in range(count)
        ]
        far.append(lax.ppermute(half if last else shard, ("seq", "head"), route))
    return far


def swap_in_pairs(far, count):
    slabs = lax.axis_size("seq")
    if not is_paired(count, slabs):
        return []
    near = []
    for piece in far:
        near.append(lax.ppermute(piece, "seq", [(s, s ^ 1) for s in range(slabs)]))
    return near


def front_body(*refs):
    hist_hbm, wq_hbm, wk_hbm, wv_hbm, pad_hbm, out_hbm = refs[:6]
    q_ref, own_ref, edge_ref, half_ref = refs[6:10]
    hist, weights, pad_ref, sems = refs[10:]
    rows, _ = hist.shape
    cols = wq_hbm.shape[0]
    step = LANES
    starts = list(range(0, rows, step))[::-1]
    half = half_ref.shape[0]
    part = lax.axis_index("seq") % (out_hbm.shape[0] // half)
    moves = [(pad_hbm, pad_ref)]
    for n, source in enumerate((wq_hbm, wk_hbm, wv_hbm)):
        moves.append((source, weights.at[pl.ds(n * cols, cols)]))
    for start in starts:
        moves.append((hist_hbm.at[pl.ds(start, step)], hist.at[pl.ds(start, step)]))
    moves.append((out_hbm.at[pl.ds(pl.multiple_of(part * half, half), half)], half_ref))
    copies = [pltpu.make_async_copy(a, b, sems.at[n]) for n, (a, b) in enumerate(moves)]
    for copy in copies:
        copy.start()
    copies[0].wait()
    pad = jnp.concatenate([pad_ref[n : n + 1, :] for n in range(rows // LANES)], 1)
    flags = jnp.broadcast_to(pad, (FLAG_ROWS, rows)).astype(F32).astype(BF16)
    own_ref[2 * cols :, :] = flags
    edge_ref[2 * cols :, :] = flags[:, rows - WIN :]
    for copy in copies[1:]:
        copy.wait()
    out = dot_last(hist[...], weights[...])
    q_ref[...] = out[:, :cols].astype(BF16)
    kv = out[:, cols:].T.astype(BF16)
    own_ref[: 2 * cols, :] = kv
    edge_ref[: 2 * cols, :] = kv[:, rows - WIN :]


def front(history, w_query, w_key, w_value, pad_mask, w_out):
    rows, width = history.shape
    half = w_out.shape[0] // 2
    cols = w_query.shape[1]
    tall = 2 * cols + FLAG_ROWS
    return pl.pallas_call(
        front_body,
        name="front",
        out_shape=(
            jax.ShapeDtypeStruct((rows, cols), BF16),
            jax.ShapeDtypeStruct((tall, rows), BF16),
            jax.ShapeDtypeStruct((tall, WIN), BF16),
            jax.ShapeDtypeStruct((half, width), BF16),
        ),
        in_specs=[RAW] * 6,
        out_specs=(WHOLE,) * 4,
        scratch_shapes=[
            pltpu.VMEM((rows, width), BF16),
            pltpu.VMEM((3 * cols, width), BF16),
            pltpu.VMEM((rows // LANES, LANES), jnp.int32),
            pltpu.SemaphoreType.DMA((5 + rows // LANES,)),
        ],
        compiler_params=pltpu.CompilerParams(vmem_limit_bytes=12 * MIB),
        cost_estimate=pl.CostEstimate(flops=AHEAD, bytes_accessed=4 * rows * width, transcendentals=0),
    )(*stay(history, w_query.T, w_key.T, w_value.T, pad_mask.reshape(-1, LANES), w_out))


def prepare_body(pos_hbm, gain_hbm, ids_hbm, target_hbm, id_ref, pos_out, gain_out, target_out, gain_row, pos, ids_ref, target_ref, sems):
    rows, share = pos.shape
    here = pl.ds(0, share)
    if pos_hbm.shape[1] != share:
        here = pl.ds(pl.multiple_of(lax.axis_index("head") * share, share), share)
    moves = ((ids_hbm, ids_ref), (target_hbm, target_ref), (gain_hbm, gain_row), (pos_hbm.at[:, here], pos))
    copies = [pltpu.make_async_copy(a, b, sems.at[n]) for n, (a, b) in enumerate(moves)]
    for copy in copies:
        copy.start()
    copies[0].wait()
    copies[1].wait()
    target_out[...] = jnp.concatenate([target_ref[n : n + 1, :] for n in range(rows // LANES)], 1)
    for n in range(ids_ref.shape[0]):
        line = jnp.broadcast_to(ids_ref[n : n + 1, :], (LANES, LANES))
        id_ref[n * LANES : (n + 1) * LANES, :] = line.T
    copies[2].wait()
    copies[3].wait()
    gain = gain_row[:, here]
    gain_out[...] = gain
    pos_out[...] = (pos[...].astype(F32) * gain).T


def prepare(pos_emb, norm_gain, neg_ids, target_ids, share):
    rows, width = pos_emb.shape
    negs = neg_ids.shape[0]
    if share % LANES:
        pos_emb = lax.dynamic_slice_in_dim(pos_emb, lax.axis_index("head") * share, share, 1)
    return pl.pallas_call(
        prepare_body,
        name="prepare",
        out_shape=(
            jax.ShapeDtypeStruct((negs, LANES), jnp.int32),
            jax.ShapeDtypeStruct((share, rows), F32),
            jax.ShapeDtypeStruct((1, share), F32),
            jax.ShapeDtypeStruct((1, rows), jnp.int32),
            jax.ShapeDtypeStruct((1, width), F32),
        ),
        in_specs=[RAW] * 4,
        out_specs=(WHOLE,) * 5,
        scratch_shapes=[
            pltpu.VMEM((rows, share), BF16),
            pltpu.VMEM((negs // LANES, LANES), jnp.int32),
            pltpu.VMEM((rows // LANES, LANES), jnp.int32),
            pltpu.SemaphoreType.DMA((4,)),
        ],
        compiler_params=pltpu.CompilerParams(vmem_limit_bytes=8 * MIB),
        cost_estimate=pl.CostEstimate(flops=rows * share, bytes_accessed=2 * rows * share, transcendentals=0),
    )(*stay(pos_emb, norm_gain[None, :], neg_ids.reshape(-1, LANES), target_ids.reshape(-1, LANES)))


def attend_blocks(starts, q_ref, own_ref, prev_ref, out_ref):
    cols = q_ref.shape[1]
    step = LANES
    span = WIN + step
    at_row = lax.broadcasted_iota(jnp.int32, (step, span), 0)
    at_col = lax.broadcasted_iota(jnp.int32, (step, span), 1)
    near = (at_col > at_row) & (at_col <= at_row + WIN)
    self_pos = at_col == at_row + WIN

    def window(lo, hi, first):
        parts = []
        if first < WIN:
            parts.append(prev_ref[lo:hi, first:WIN])
        last = first + span
        if last > WIN:
            parts.append(own_ref[lo:hi, max(first - WIN, 0) : last - WIN])
        return parts[0] if len(parts) == 1 else jnp.concatenate(parts, 1)

    for start in starts:
        flags = window(2 * cols, 2 * cols + FLAG_ROWS, start).astype(F32)[:1]
        allowed = near & ((flags == 1.0) | self_pos)
        for head in range(cols // HD):
            lo = head * HD
            scores = dot_plain(q_ref[start : start + step, lo : lo + HD], window(lo, lo + HD, start)) * HD**-0.5
            scores = jnp.where(allowed, scores, LOW)
            top = jnp.max(scores, 1, keepdims=True)
            weights = jnp.where(allowed, jnp.exp(scores - top), 0.0)
            prob = (weights / jnp.sum(weights, 1, keepdims=True)).astype(BF16)
            value = window(cols + lo, cols + lo + HD, start)
            at = start - starts[0]
            out_ref[lo : lo + HD, at : at + step] = dot_last(value, prob).astype(BF16)


def attend_late_body(q_ref, own_ref, out_ref):
    rows = q_ref.shape[0]
    attend_blocks(range(WIN, rows, LANES), q_ref, own_ref, None, out_ref)


def attend_early_body(q_ref, own_ref, prev_ref, late_ref, out_ref):
    out_ref[:, WIN:] = late_ref[...]
    attend_blocks(range(0, WIN, LANES), q_ref, own_ref, prev_ref, out_ref)


def attend(body, width, *arrays):
    rows, cols = arrays[0].shape
    return pl.pallas_call(
        body,
        out_shape=jax.ShapeDtypeStruct((cols, width), BF16),
        in_specs=[WHOLE] * len(arrays),
        out_specs=WHOLE,
        compiler_params=pltpu.CompilerParams(vmem_limit_bytes=8 * MIB),
        cost_estimate=pl.CostEstimate(flops=AHEAD, bytes_accessed=6 * rows * cols, transcendentals=rows * WIN),
    )(*arrays)


def premix_body(count, split, neg_ref, gain_ref, own_ref, *refs):
    far, near, (mix_ref, turned_ref, scaled, held) = refs[:split[0]], refs[split[0] : sum(split)], refs[sum(split) :]
    total, width = neg_ref.shape
    tall = own_ref.shape[0]
    block = 256
    gain = gain_ref[...]
    first = lax.axis_index("seq") % 2 == 0
    pieces = [own_ref]
    for k in range(1, count):
        if not near:
            pieces.append(far[k - 1])
            continue
        mine, theirs = far[(k - 1) // 2][...], near[(k - 1) // 2][...]
        even, odd = jnp.where(first, mine, theirs), jnp.where(first, theirs, mine)
        held[k - 1] = jnp.concatenate([even, odd], 0) if k == count - 1 else even if k % 2 else odd
        pieces.append(held.at[k - 1])
    for k in range(count):
        scaled[k * tall : (k + 1) * tall, :] = (pieces[k][...].astype(F32) * gain).astype(BF16)
    turn = width // (total // block)
    for n, start in enumerate(range(0, total, block)):
        part = neg_ref[start : start + block, :]
        mix_ref[start : start + block, :] = dot_last(part, scaled[...]).astype(BF16)
        cols = slice(n * turn, (n + 1) * turn)
        whole = jnp.concatenate([ref[:, cols].astype(F32) for ref in pieces], 0)
        turned_ref[cols, :] = whole.T.astype(BF16)


def premix(neg_emb, gain_row, own, far, near):
    negs, width = neg_emb.shape
    count = lax.axis_size("head")
    tall = own.shape[0]
    deep = count * tall
    return pl.pallas_call(
        functools.partial(premix_body, count, (len(far), len(near))),
        name="premix",
        out_shape=(
            jax.ShapeDtypeStruct((negs, deep), BF16),
            jax.ShapeDtypeStruct((width, deep), BF16),
        ),
        in_specs=[WHOLE] * (3 + len(far) + len(near)),
        out_specs=(WHOLE, WHOLE),
        scratch_shapes=[pltpu.VMEM((deep, width), BF16), pltpu.VMEM((count - 1, tall, width), BF16)],
        compiler_params=pltpu.CompilerParams(vmem_limit_bytes=20 * MIB),
        cost_estimate=pl.CostEstimate(flops=2 * negs * width * deep, bytes_accessed=2 * negs * width, transcendentals=0),
    )(neg_emb, gain_row, own, *far, *near)


def score_body(count, *refs):
    o_refs = refs[:count]
    mix_ref, turned_ref, id_ref, pos_ref, target_ref, stat_ref, user_ref, attn, logits = refs[count:]
    width, rows = attn.shape
    share = user_ref.shape[0]
    negs = mix_ref.shape[0]
    block = 256
    heads = jnp.concatenate([ref[...] for ref in o_refs], 0)
    total = jnp.zeros((8, rows), F32)
    for start in range(0, width, block):
        part = dot_plain(turned_ref[start : start + block, :], heads)
        attn[start : start + block, :] = part
        total += jnp.sum((part * part).reshape(block // 8, 8, rows), 0)
    scale = lax.rsqrt(jnp.sum(total, 0, keepdims=True) / width + 1e-05)
    here = pl.multiple_of(lax.axis_index("head") * share, share)
    user = attn[pl.ds(here, share), :] * scale
    user_ref[...] = user
    pos = jnp.sum(user * pos_ref[...], 0, keepdims=True)
    target = target_ref[...]
    top = jnp.full((8, rows), LOW, F32)
    for start in range(0, negs, block):
        part = dot_plain(mix_ref[start : start + block, :], heads) * scale
        ids = id_ref[start : start + block, :]
        hit = jnp.concatenate([ids] * (rows // LANES), 1) == target
        part = jnp.where(hit, LOW, part)
        logits[start : start + block, :] = part
        top = jnp.maximum(top, jnp.max(part.reshape(block // 8, 8, rows), 0))
    top = jnp.max(top, 0, keepdims=True)
    mass = jnp.zeros((8, rows), F32)
    for start in range(0, negs, block):
        part = jnp.exp(logits[start : start + block, :] - top)
        mass += jnp.sum(part.reshape(block // 8, 8, rows), 0)
    mass = jnp.sum(mass, 0, keepdims=True)
    stat_ref[...] = jnp.concatenate([top, mass, pos, pos], 0)


def score(heads, mix, turned, id_cols, pos_turned, target):
    count = len(heads)
    negs, deep = mix.shape
    width = turned.shape[0]
    share, rows = pos_turned.shape
    return pl.pallas_call(
        functools.partial(score_body, count),
        name="score",
        out_shape=(
            jax.ShapeDtypeStruct((4, rows), F32),
            jax.ShapeDtypeStruct((share, rows), F32),
        ),
        in_specs=[WHOLE] * (count + 5),
        out_specs=(WHOLE, WHOLE),
        scratch_shapes=[pltpu.VMEM((width, rows), F32), pltpu.VMEM((negs, rows), F32)],
        compiler_params=pltpu.CompilerParams(vmem_limit_bytes=28 * MIB),
        cost_estimate=pl.CostEstimate(flops=2 * rows * deep * (negs + width), bytes_accessed=2 * negs * deep, transcendentals=negs * rows),
    )(*heads, mix, turned, id_cols, pos_turned, target)


def finish_body(user_ref, gain_ref, out_ref):
    out_ref[...] = (user_ref[...].T * gain_ref[...]).astype(BF16)


def finish(user, gain_here):
    share, rows = user.shape
    return pl.pallas_call(
        finish_body,
        name="finish",
        out_shape=jax.ShapeDtypeStruct((rows, share), BF16),
        in_specs=[WHOLE, WHOLE],
        out_specs=WHOLE,
        compiler_params=pltpu.CompilerParams(vmem_limit_bytes=8 * MIB),
        cost_estimate=pl.CostEstimate(flops=2 * rows * share, bytes_accessed=6 * rows * share, transcendentals=0),
    )(user, gain_here)


def on_device(
    history,
    w_query,
    w_key,
    w_value,
    w_out,
    norm_gain,
    neg_emb,
    pos_emb,
    neg_ids,
    target_ids,
    pad_mask,
):
    width = history.shape[1]
    count = lax.axis_size("head")
    query, own, edge, half = front(history, w_query, w_key, w_value, pad_mask, w_out)
    prev = from_behind(edge, "seq", 1)
    far = fetch_in_pairs(w_out, half)
    late = attend(attend_late_body, history.shape[0] - WIN, query, own)
    mine = attend(attend_early_body, history.shape[0], query, own, prev, late)
    heads = from_all(mine, "head")
    id_cols, pos_turned, gain_here, target, gain_row = prepare(pos_emb, norm_gain, neg_ids, target_ids, width // count)
    near = swap_in_pairs(far, count)
    mix, turned = premix(neg_emb, gain_row, w_out, far, near)
    stats, user = score(heads, mix, turned, id_cols, pos_turned, target)
    all_stats = from_all(stats, "head")
    user_share = finish(user, gain_here)
    pos_logit = functools.reduce(jnp.add, [s[2] for s in all_stats])
    upper = functools.reduce(jnp.maximum, [s[0] for s in all_stats], pos_logit)
    total = functools.reduce(jnp.add, [s[1] * jnp.exp(s[0] - upper) for s in all_stats])
    loss = upper + jnp.log(total + jnp.exp(pos_logit - upper)) - pos_logit
    return (user_share, loss)


def solution(mesh):
    return jax.shard_map(
        on_device,
        mesh=mesh,
        in_specs=(
            P("seq", None),
            P(None, "head"),
            P(None, "head"),
            P(None, "head"),
            P("head", None),
            P(),
            P("head", None),
            P("seq", None),
            P("head"),
            P("seq"),
            P("seq"),
        ),
        out_specs=(P("seq", "head"), P("seq")),
        check_vma=False,
    )
```

```python
import functools

import jax
import jax.numpy as jnp
from jax import lax
from jax.experimental import pallas as pl
from jax.experimental.pallas import tpu as pltpu
from jax.sharding import PartitionSpec as P


HD = 64
WIN = 256
LANES = 128
FLAG_ROWS = 16
LOW = -1e30
MIB = 1 << 20
AHEAD = 4 * 10**9
F32 = jnp.float32
BF16 = jnp.bfloat16
WHOLE = pl.BlockSpec(memory_space=pltpu.VMEM)
RAW = pl.BlockSpec(memory_space=pltpu.HBM)


def stay(*arrays):
    return [pltpu.with_memory_space_constraint(a, pltpu.HBM) for a in arrays]


def dot_last(a, b):
    return lax.dot_general(a, b, (((1,), (1,)), ((), ())), preferred_element_type=F32)


def dot_plain(a, b):
    return lax.dot_general(a, b, (((1,), (0,)), ((), ())), preferred_element_type=F32)


def from_behind(shard, axis):
    count = lax.axis_size(axis)
    return lax.ppermute(shard, axis, [(i, (i + 1) % count) for i in range(count)])


def partners(axis):
    count = lax.axis_size(axis)
    if count & (count - 1) == 0:
        return [[(i, i ^ k) for i in range(count)] for k in range(1, count)]
    return [[(i, (i + k) % count) for i in range(count)] for k in range(1, count)]


def from_all(shard, axis):
    pieces = [shard]
    for pairs in partners(axis):
        pieces.append(lax.ppermute(shard, axis, pairs))
    return pieces


def is_paired(count, slabs):
    return count & (count - 1) == 0 and slabs % 2 == 0


def fetch_in_pairs(shard, half):
    count, slabs = lax.axis_size("head"), lax.axis_size("seq")
    if not is_paired(count, slabs):
        return from_all(shard, "head")[1:]
    far = []
    for odd in range(1, count, 2):
        last = odd + 1 == count
        route = [
            (s * count + h, s * count + (h ^ (odd if last else odd + s % 2)))
            for s in range(slabs)
            for h in range(count)
        ]
        far.append(lax.ppermute(half if last else shard, ("seq", "head"), route))
    return far


def swap_in_pairs(far, count):
    slabs = lax.axis_size("seq")
    if not is_paired(count, slabs):
        return []
    near = []
    for piece in far:
        near.append(lax.ppermute(piece, "seq", [(s, s ^ 1) for s in range(slabs)]))
    return near


def front_body(*refs):
    hist_hbm, wq_hbm, wk_hbm, wv_hbm, pad_hbm, out_hbm = refs[:6]
    q_ref, own_ref, edge_ref, half_ref = refs[6:10]
    hist, weights, pad_ref, sems = refs[10:]
    rows, _ = hist.shape
    cols = wq_hbm.shape[0]
    step = LANES
    starts = list(range(0, rows, step))[::-1]
    half = half_ref.shape[0]
    part = lax.axis_index("seq") % (out_hbm.shape[0] // half)
    moves = [(pad_hbm, pad_ref)]
    for n, source in enumerate((wq_hbm, wk_hbm, wv_hbm)):
        moves.append((source, weights.at[pl.ds(n * cols, cols)]))
    for start in starts:
        moves.append((hist_hbm.at[pl.ds(start, step)], hist.at[pl.ds(start, step)]))
    moves.append((out_hbm.at[pl.ds(pl.multiple_of(part * half, half), half)], half_ref))
    copies = [pltpu.make_async_copy(a, b, sems.at[n]) for n, (a, b) in enumerate(moves)]
    for copy in copies:
        copy.start()
    copies[0].wait()
    pad = jnp.concatenate([pad_ref[n : n + 1, :] for n in range(rows // LANES)], 1)
    flags = jnp.broadcast_to(pad, (FLAG_ROWS, rows)).astype(F32).astype(BF16)
    own_ref[2 * cols :, :] = flags
    edge_ref[2 * cols :, :] = flags[:, rows - WIN :]
    for copy in copies[1:]:
        copy.wait()
    out = dot_last(hist[...], weights[...])
    q_ref[...] = out[:, :cols].astype(BF16)
    kv = out[:, cols:].T.astype(BF16)
    own_ref[: 2 * cols, :] = kv
    edge_ref[: 2 * cols, :] = kv[:, rows - WIN :]


def front(history, w_query, w_key, w_value, pad_mask, w_out):
    rows, width = history.shape
    half = w_out.shape[0] // 2
    cols = w_query.shape[1]
    tall = 2 * cols + FLAG_ROWS
    return pl.pallas_call(
        front_body,
        name="front",
        out_shape=(
            jax.ShapeDtypeStruct((rows, cols), BF16),
            jax.ShapeDtypeStruct((tall, rows), BF16),
            jax.ShapeDtypeStruct((tall, WIN), BF16),
            jax.ShapeDtypeStruct((half, width), BF16),
        ),
        in_specs=[RAW] * 6,
        out_specs=(WHOLE,) * 4,
        scratch_shapes=[
            pltpu.VMEM((rows, width), BF16),
            pltpu.VMEM((3 * cols, width), BF16),
            pltpu.VMEM((rows // LANES, LANES), jnp.int32),
            pltpu.SemaphoreType.DMA((5 + rows // LANES,)),
        ],
        compiler_params=pltpu.CompilerParams(vmem_limit_bytes=12 * MIB),
        cost_estimate=pl.CostEstimate(flops=AHEAD, bytes_accessed=4 * rows * width, transcendentals=0),
    )(*stay(history, w_query.T, w_key.T, w_value.T, pad_mask.reshape(-1, LANES), w_out))


def prepare_body(pos_hbm, gain_hbm, ids_hbm, target_hbm, id_ref, pos_out, gain_out, target_out, gain_row, pos, ids_ref, target_ref, sems):
    rows, share = pos.shape
    here = pl.ds(0, share)
    if pos_hbm.shape[1] != share:
        here = pl.ds(pl.multiple_of(lax.axis_index("head") * share, share), share)
    moves = ((ids_hbm, ids_ref), (target_hbm, target_ref), (gain_hbm, gain_row), (pos_hbm.at[:, here], pos))
    copies = [pltpu.make_async_copy(a, b, sems.at[n]) for n, (a, b) in enumerate(moves)]
    for copy in copies:
        copy.start()
    copies[0].wait()
    copies[1].wait()
    target_out[...] = jnp.concatenate([target_ref[n : n + 1, :] for n in range(rows // LANES)], 1)
    for n in range(ids_ref.shape[0]):
        line = jnp.broadcast_to(ids_ref[n : n + 1, :], (LANES, LANES))
        id_ref[n * LANES : (n + 1) * LANES, :] = line.T
    copies[2].wait()
    copies[3].wait()
    gain = gain_row[:, here]
    gain_out[...] = gain
    pos_out[...] = (pos[...].astype(F32) * gain).T


def prepare(pos_emb, norm_gain, neg_ids, target_ids, share):
    rows, width = pos_emb.shape
    negs = neg_ids.shape[0]
    if share % LANES:
        pos_emb = lax.dynamic_slice_in_dim(pos_emb, lax.axis_index("head") * share, share, 1)
    return pl.pallas_call(
        prepare_body,
        name="prepare",
        out_shape=(
            jax.ShapeDtypeStruct((negs, LANES), jnp.int32),
            jax.ShapeDtypeStruct((share, rows), F32),
            jax.ShapeDtypeStruct((1, share), F32),
            jax.ShapeDtypeStruct((1, rows), jnp.int32),
            jax.ShapeDtypeStruct((1, width), F32),
        ),
        in_specs=[RAW] * 4,
        out_specs=(WHOLE,) * 5,
        scratch_shapes=[
            pltpu.VMEM((rows, share), BF16),
            pltpu.VMEM((negs // LANES, LANES), jnp.int32),
            pltpu.VMEM((rows // LANES, LANES), jnp.int32),
            pltpu.SemaphoreType.DMA((4,)),
        ],
        compiler_params=pltpu.CompilerParams(vmem_limit_bytes=8 * MIB),
        cost_estimate=pl.CostEstimate(flops=rows * share, bytes_accessed=2 * rows * share, transcendentals=0),
    )(*stay(pos_emb, norm_gain[None, :], neg_ids.reshape(-1, LANES), target_ids.reshape(-1, LANES)))


def attend_blocks(starts, q_ref, own_ref, prev_ref, out_ref):
    cols = q_ref.shape[1]
    step = LANES
    span = WIN + step
    at_row = lax.broadcasted_iota(jnp.int32, (step, span), 0)
    at_col = lax.broadcasted_iota(jnp.int32, (step, span), 1)
    near = (at_col > at_row) & (at_col <= at_row + WIN)
    self_pos = at_col == at_row + WIN
    inside = lax.axis_index("seq") > 0

    def window(lo, hi, first):
        parts = []
        if first < WIN:
            parts.append(prev_ref[lo:hi, first:WIN])
        last = first + span
        if last > WIN:
            parts.append(own_ref[lo:hi, max(first - WIN, 0) : last - WIN])
        return parts[0] if len(parts) == 1 else jnp.concatenate(parts, 1)

    for start in starts:
        flags = window(2 * cols, 2 * cols + FLAG_ROWS, start).astype(F32)[:1]
        allowed = near & ((flags == 1.0) | self_pos)
        if start < WIN:
            allowed = allowed & ((at_col >= WIN - start) | inside)
        for head in range(cols // HD):
            lo = head * HD
            scores = dot_plain(q_ref[start : start + step, lo : lo + HD], window(lo, lo + HD, start)) * HD**-0.5
            scores = jnp.where(allowed, scores, LOW)
            top = jnp.max(scores, 1, keepdims=True)
            weights = jnp.where(allowed, jnp.exp(scores - top), 0.0)
            prob = (weights / jnp.sum(weights, 1, keepdims=True)).astype(BF16)
            value = window(cols + lo, cols + lo + HD, start)
            at = start - starts[0]
            out_ref[lo : lo + HD, at : at + step] = dot_last(value, prob).astype(BF16)


def attend_late_body(q_ref, own_ref, out_ref):
    rows = q_ref.shape[0]
    attend_blocks(range(WIN, rows, LANES), q_ref, own_ref, None, out_ref)


def attend_early_body(q_ref, own_ref, prev_ref, late_ref, out_ref):
    out_ref[:, WIN:] = late_ref[...]
    attend_blocks(range(0, WIN, LANES), q_ref, own_ref, prev_ref, out_ref)


def attend(body, width, *arrays):
    rows, cols = arrays[0].shape
    return pl.pallas_call(
        body,
        out_shape=jax.ShapeDtypeStruct((cols, width), BF16),
        in_specs=[WHOLE] * len(arrays),
        out_specs=WHOLE,
        compiler_params=pltpu.CompilerParams(vmem_limit_bytes=8 * MIB),
        cost_estimate=pl.CostEstimate(flops=AHEAD, bytes_accessed=6 * rows * cols, transcendentals=rows * WIN),
    )(*arrays)


def premix_body(count, split, neg_ref, gain_ref, own_ref, *refs):
    far, near, (mix_ref, turned_ref, scaled, held) = refs[:split[0]], refs[split[0] : sum(split)], refs[sum(split) :]
    total, width = neg_ref.shape
    tall = own_ref.shape[0]
    block = 256
    gain = gain_ref[...]
    first = lax.axis_index("seq") % 2 == 0
    pieces = [own_ref]
    for k in range(1, count):
        if not near:
            pieces.append(far[k - 1])
            continue
        mine, theirs = far[(k - 1) // 2][...], near[(k - 1) // 2][...]
        even, odd = jnp.where(first, mine, theirs), jnp.where(first, theirs, mine)
        held[k - 1] = jnp.concatenate([even, odd], 0) if k == count - 1 else even if k % 2 else odd
        pieces.append(held.at[k - 1])
    for k in range(count):
        scaled[k * tall : (k + 1) * tall, :] = (pieces[k][...].astype(F32) * gain).astype(BF16)
    turn = width // (total // block)
    for n, start in enumerate(range(0, total, block)):
        part = neg_ref[start : start + block, :]
        mix_ref[start : start + block, :] = dot_last(part, scaled[...]).astype(BF16)
        cols = slice(n * turn, (n + 1) * turn)
        whole = jnp.concatenate([ref[:, cols].astype(F32) for ref in pieces], 0)
        turned_ref[cols, :] = whole.T.astype(BF16)


def premix(neg_emb, gain_row, own, far, near):
    negs, width = neg_emb.shape
    count = lax.axis_size("head")
    tall = own.shape[0]
    deep = count * tall
    return pl.pallas_call(
        functools.partial(premix_body, count, (len(far), len(near))),
        name="premix",
        out_shape=(
            jax.ShapeDtypeStruct((negs, deep), BF16),
            jax.ShapeDtypeStruct((width, deep), BF16),
        ),
        in_specs=[WHOLE] * (3 + len(far) + len(near)),
        out_specs=(WHOLE, WHOLE),
        scratch_shapes=[pltpu.VMEM((deep, width), BF16), pltpu.VMEM((count - 1, tall, width), BF16)],
        compiler_params=pltpu.CompilerParams(vmem_limit_bytes=20 * MIB),
        cost_estimate=pl.CostEstimate(flops=2 * negs * width * deep, bytes_accessed=2 * negs * width, transcendentals=0),
    )(neg_emb, gain_row, own, *far, *near)


def score_body(count, *refs):
    o_refs = refs[:count]
    mix_ref, turned_ref, id_ref, pos_ref, target_ref, stat_ref, user_ref, attn, logits = refs[count:]
    width, rows = attn.shape
    share = user_ref.shape[0]
    negs = mix_ref.shape[0]
    block = 256
    heads = jnp.concatenate([ref[...] for ref in o_refs], 0)
    total = jnp.zeros((8, rows), F32)
    for start in range(0, width, block):
        part = dot_plain(turned_ref[start : start + block, :], heads)
        attn[start : start + block, :] = part
        total += jnp.sum((part * part).reshape(block // 8, 8, rows), 0)
    scale = lax.rsqrt(jnp.sum(total, 0, keepdims=True) / width + 1e-05)
    here = pl.multiple_of(lax.axis_index("head") * share, share)
    user = attn[pl.ds(here, share), :] * scale
    user_ref[...] = user
    pos = jnp.sum(user * pos_ref[...], 0, keepdims=True)
    target = target_ref[...]
    top = jnp.full((8, rows), LOW, F32)
    for start in range(0, negs, block):
        part = dot_plain(mix_ref[start : start + block, :], heads) * scale
        ids = id_ref[start : start + block, :]
        hit = jnp.concatenate([ids] * (rows // LANES), 1) == target
        part = jnp.where(hit, LOW, part)
        logits[start : start + block, :] = part
        top = jnp.maximum(top, jnp.max(part.reshape(block // 8, 8, rows), 0))
    top = jnp.max(top, 0, keepdims=True)
    mass = jnp.zeros((8, rows), F32)
    for start in range(0, negs, block):
        part = jnp.exp(logits[start : start + block, :] - top)
        mass += jnp.sum(part.reshape(block // 8, 8, rows), 0)
    mass = jnp.sum(mass, 0, keepdims=True)
    stat_ref[...] = jnp.concatenate([top, mass, pos, pos], 0)


def score(heads, mix, turned, id_cols, pos_turned, target):
    count = len(heads)
    negs, deep = mix.shape
    width = turned.shape[0]
    share, rows = pos_turned.shape
    return pl.pallas_call(
        functools.partial(score_body, count),
        name="score",
        out_shape=(
            jax.ShapeDtypeStruct((4, rows), F32),
            jax.ShapeDtypeStruct((share, rows), F32),
        ),
        in_specs=[WHOLE] * (count + 5),
        out_specs=(WHOLE, WHOLE),
        scratch_shapes=[pltpu.VMEM((width, rows), F32), pltpu.VMEM((negs, rows), F32)],
        compiler_params=pltpu.CompilerParams(vmem_limit_bytes=28 * MIB),
        cost_estimate=pl.CostEstimate(flops=2 * rows * deep * (negs + width), bytes_accessed=2 * negs * deep, transcendentals=negs * rows),
    )(*heads, mix, turned, id_cols, pos_turned, target)


def finish_body(user_ref, gain_ref, out_ref):
    out_ref[...] = (user_ref[...].T * gain_ref[...]).astype(BF16)


def finish(user, gain_here):
    share, rows = user.shape
    return pl.pallas_call(
        finish_body,
        name="finish",
        out_shape=jax.ShapeDtypeStruct((rows, share), BF16),
        in_specs=[WHOLE, WHOLE],
        out_specs=WHOLE,
        compiler_params=pltpu.CompilerParams(vmem_limit_bytes=8 * MIB),
        cost_estimate=pl.CostEstimate(flops=2 * rows * share, bytes_accessed=6 * rows * share, transcendentals=0),
    )(user, gain_here)


def on_device(
    history,
    w_query,
    w_key,
    w_value,
    w_out,
    norm_gain,
    neg_emb,
    pos_emb,
    neg_ids,
    target_ids,
    pad_mask,
):
    width = history.shape[1]
    count = lax.axis_size("head")
    query, own, edge, half = front(history, w_query, w_key, w_value, pad_mask, w_out)
    prev = from_behind(edge, "seq")
    far = fetch_in_pairs(w_out, half)
    late = attend(attend_late_body, history.shape[0] - WIN, query, own)
    mine = attend(attend_early_body, history.shape[0], query, own, prev, late)
    heads = from_all(mine, "head")
    id_cols, pos_turned, gain_here, target, gain_row = prepare(pos_emb, norm_gain, neg_ids, target_ids, width // count)
    near = swap_in_pairs(far, count)
    mix, turned = premix(neg_emb, gain_row, w_out, far, near)
    stats, user = score(heads, mix, turned, id_cols, pos_turned, target)
    all_stats = from_all(stats, "head")
    user_share = finish(user, gain_here)
    pos_logit = functools.reduce(jnp.add, [s[2] for s in all_stats])
    upper = functools.reduce(jnp.maximum, [s[0] for s in all_stats], pos_logit)
    total = functools.reduce(jnp.add, [s[1] * jnp.exp(s[0] - upper) for s in all_stats])
    loss = upper + jnp.log(total + jnp.exp(pos_logit - upper)) - pos_logit
    return (user_share, loss)


def solution(mesh):
    return jax.shard_map(
        on_device,
        mesh=mesh,
        in_specs=(
            P("seq", None),
            P(None, "head"),
            P(None, "head"),
            P(None, "head"),
            P("head", None),
            P(),
            P("head", None),
            P("seq", None),
            P("head"),
            P("seq"),
            P("seq"),
        ),
        out_specs=(P("seq", "head"), P("seq")),
        check_vma=False,
    )
```

```python
import functools

import jax
import jax.numpy as jnp
from jax import lax
from jax.experimental import pallas as pl
from jax.experimental.pallas import tpu as pltpu
from jax.sharding import PartitionSpec as P


HD = 64
WIN = 256
LANES = 128
FLAG_ROWS = 16
LOW = -1e30
LOG2E = 1.4426950408889634
MIB = 1 << 20
AHEAD = 4 * 10**9
F32 = jnp.float32
BF16 = jnp.bfloat16
WHOLE = pl.BlockSpec(memory_space=pltpu.VMEM)
RAW = pl.BlockSpec(memory_space=pltpu.HBM)


def stay(*arrays):
    return [pltpu.with_memory_space_constraint(a, pltpu.HBM) for a in arrays]


def dot_last(a, b):
    return lax.dot_general(a, b, (((1,), (1,)), ((), ())), preferred_element_type=F32)


def dot_plain(a, b):
    return lax.dot_general(a, b, (((1,), (0,)), ((), ())), preferred_element_type=F32)


def from_behind(shard, axis):
    count = lax.axis_size(axis)
    return lax.ppermute(shard, axis, [(i, (i + 1) % count) for i in range(count)])


def partners(axis):
    count = lax.axis_size(axis)
    if count & (count - 1) == 0:
        return [[(i, i ^ k) for i in range(count)] for k in range(1, count)]
    return [[(i, (i + k) % count) for i in range(count)] for k in range(1, count)]


def from_all(shard, axis):
    pieces = [shard]
    for pairs in partners(axis):
        pieces.append(lax.ppermute(shard, axis, pairs))
    return pieces


def is_paired(count, slabs):
    return count & (count - 1) == 0 and slabs % 2 == 0


def fetch_in_pairs(shard, half):
    count, slabs = lax.axis_size("head"), lax.axis_size("seq")
    if not is_paired(count, slabs):
        return from_all(shard, "head")[1:]
    far = []
    for odd in range(1, count, 2):
        last = odd + 1 == count
        route = [
            (s * count + h, s * count + (h ^ (odd if last else odd + s % 2)))
            for s in range(slabs)
            for h in range(count)
        ]
        far.append(lax.ppermute(half if last else shard, ("seq", "head"), route))
    return far


def swap_in_pairs(far, count):
    slabs = lax.axis_size("seq")
    if not is_paired(count, slabs):
        return []
    near = []
    for piece in far:
        near.append(lax.ppermute(piece, "seq", [(s, s ^ 1) for s in range(slabs)]))
    return near


def front_body(*refs):
    hist_hbm, wq_hbm, wk_hbm, wv_hbm, pad_hbm, out_hbm = refs[:6]
    q_ref, own_ref, edge_ref, half_ref = refs[6:10]
    hist, weights, pad_ref, sems = refs[10:]
    rows, _ = hist.shape
    cols = wq_hbm.shape[0]
    step = LANES
    starts = list(range(0, rows, step))[::-1]
    half = half_ref.shape[0]
    part = lax.axis_index("seq") % (out_hbm.shape[0] // half)
    moves = [(pad_hbm, pad_ref)]
    for n, source in enumerate((wq_hbm, wk_hbm, wv_hbm)):
        moves.append((source, weights.at[pl.ds(n * cols, cols)]))
    for start in starts:
        moves.append((hist_hbm.at[pl.ds(start, step)], hist.at[pl.ds(start, step)]))
    moves.append((out_hbm.at[pl.ds(pl.multiple_of(part * half, half), half)], half_ref))
    copies = [pltpu.make_async_copy(a, b, sems.at[n]) for n, (a, b) in enumerate(moves)]
    for copy in copies:
        copy.start()
    copies[0].wait()
    pad = jnp.concatenate([pad_ref[n : n + 1, :] for n in range(rows // LANES)], 1)
    flags = jnp.broadcast_to(pad, (FLAG_ROWS, rows)).astype(F32).astype(BF16)
    own_ref[2 * cols :, :] = flags
    edge_ref[2 * cols :, :] = flags[:, rows - WIN :]
    for copy in copies[1:]:
        copy.wait()
    out = dot_last(hist[...], weights[...])
    q_ref[...] = out[:, :cols].astype(BF16)
    kv = out[:, cols:].T.astype(BF16)
    own_ref[: 2 * cols, :] = kv
    edge_ref[: 2 * cols, :] = kv[:, rows - WIN :]


def front(history, w_query, w_key, w_value, pad_mask, w_out):
    rows, width = history.shape
    half = w_out.shape[0] // 2
    cols = w_query.shape[1]
    tall = 2 * cols + FLAG_ROWS
    return pl.pallas_call(
        front_body,
        name="front",
        out_shape=(
            jax.ShapeDtypeStruct((rows, cols), BF16),
            jax.ShapeDtypeStruct((tall, rows), BF16),
            jax.ShapeDtypeStruct((tall, WIN), BF16),
            jax.ShapeDtypeStruct((half, width), BF16),
        ),
        in_specs=[RAW] * 6,
        out_specs=(WHOLE,) * 4,
        scratch_shapes=[
            pltpu.VMEM((rows, width), BF16),
            pltpu.VMEM((3 * cols, width), BF16),
            pltpu.VMEM((rows // LANES, LANES), jnp.int32),
            pltpu.SemaphoreType.DMA((5 + rows // LANES,)),
        ],
        compiler_params=pltpu.CompilerParams(vmem_limit_bytes=12 * MIB),
        cost_estimate=pl.CostEstimate(flops=AHEAD, bytes_accessed=4 * rows * width, transcendentals=0),
    )(*stay(history, w_query.T, w_key.T, w_value.T, pad_mask.reshape(-1, LANES), w_out))


def prepare_body(pos_hbm, gain_hbm, ids_hbm, target_hbm, id_ref, pos_out, gain_out, target_out, gain_row, pos, ids_ref, target_ref, sems):
    rows, share = pos.shape
    here = pl.ds(0, share)
    if pos_hbm.shape[1] != share:
        here = pl.ds(pl.multiple_of(lax.axis_index("head") * share, share), share)
    moves = ((ids_hbm, ids_ref), (target_hbm, target_ref), (gain_hbm, gain_row), (pos_hbm.at[:, here], pos))
    copies = [pltpu.make_async_copy(a, b, sems.at[n]) for n, (a, b) in enumerate(moves)]
    for copy in copies:
        copy.start()
    copies[0].wait()
    copies[1].wait()
    target_out[...] = jnp.concatenate([target_ref[n : n + 1, :] for n in range(rows // LANES)], 1)
    for n in range(ids_ref.shape[0]):
        line = jnp.broadcast_to(ids_ref[n : n + 1, :], (LANES, LANES))
        id_ref[n * LANES : (n + 1) * LANES, :] = line.T
    copies[2].wait()
    copies[3].wait()
    gain = gain_row[:, here]
    gain_out[...] = gain
    pos_out[...] = (pos[...].astype(F32) * gain).T


def prepare(pos_emb, norm_gain, neg_ids, target_ids, share):
    rows, width = pos_emb.shape
    negs = neg_ids.shape[0]
    if share % LANES:
        pos_emb = lax.dynamic_slice_in_dim(pos_emb, lax.axis_index("head") * share, share, 1)
    return pl.pallas_call(
        prepare_body,
        name="prepare",
        out_shape=(
            jax.ShapeDtypeStruct((negs, LANES), jnp.int32),
            jax.ShapeDtypeStruct((share, rows), F32),
            jax.ShapeDtypeStruct((1, share), F32),
            jax.ShapeDtypeStruct((1, rows), jnp.int32),
            jax.ShapeDtypeStruct((1, width), F32),
        ),
        in_specs=[RAW] * 4,
        out_specs=(WHOLE,) * 5,
        scratch_shapes=[
            pltpu.VMEM((rows, share), BF16),
            pltpu.VMEM((negs // LANES, LANES), jnp.int32),
            pltpu.VMEM((rows // LANES, LANES), jnp.int32),
            pltpu.SemaphoreType.DMA((4,)),
        ],
        compiler_params=pltpu.CompilerParams(vmem_limit_bytes=8 * MIB),
        cost_estimate=pl.CostEstimate(flops=rows * share, bytes_accessed=2 * rows * share, transcendentals=0),
    )(*stay(pos_emb, norm_gain[None, :], neg_ids.reshape(-1, LANES), target_ids.reshape(-1, LANES)))


def attend_blocks(starts, q_ref, own_ref, prev_ref, out_ref):
    cols = q_ref.shape[1]
    step = LANES
    span = WIN + step
    at_row = lax.broadcasted_iota(jnp.int32, (step, span), 0)
    at_col = lax.broadcasted_iota(jnp.int32, (step, span), 1)
    near = (at_col > at_row) & (at_col <= at_row + WIN)
    self_pos = at_col == at_row + WIN
    inside = lax.axis_index("seq") > 0

    def window(lo, hi, first):
        parts = []
        if first < WIN:
            parts.append(prev_ref[lo:hi, first:WIN])
        last = first + span
        if last > WIN:
            parts.append(own_ref[lo:hi, max(first - WIN, 0) : last - WIN])
        return parts[0] if len(parts) == 1 else jnp.concatenate(parts, 1)

    for start in starts:
        flags = window(2 * cols, 2 * cols + FLAG_ROWS, start).astype(F32)[:1]
        allowed = near & ((flags == 1.0) | self_pos)
        if start < WIN:
            allowed = allowed & ((at_col >= WIN - start) | inside)
        for head in range(cols // HD):
            lo = head * HD
            scores = dot_plain(q_ref[start : start + step, lo : lo + HD], window(lo, lo + HD, start)) * HD**-0.5
            scores = jnp.where(allowed, scores, LOW)
            top = jnp.max(scores, 1, keepdims=True)
            weights = jnp.where(allowed, jnp.exp(scores - top), 0.0)
            prob = (weights / jnp.sum(weights, 1, keepdims=True)).astype(BF16)
            value = window(cols + lo, cols + lo + HD, start)
            at = start - starts[0]
            out_ref[lo : lo + HD, at : at + step] = dot_last(value, prob).astype(BF16)


def attend_late_body(q_ref, own_ref, out_ref):
    rows = q_ref.shape[0]
    attend_blocks(range(WIN, rows, LANES), q_ref, own_ref, None, out_ref)


def attend_early_body(q_ref, own_ref, prev_ref, late_ref, out_ref):
    out_ref[:, WIN:] = late_ref[...]
    attend_blocks(range(0, WIN, LANES), q_ref, own_ref, prev_ref, out_ref)


def attend(body, width, *arrays):
    rows, cols = arrays[0].shape
    return pl.pallas_call(
        body,
        out_shape=jax.ShapeDtypeStruct((cols, width), BF16),
        in_specs=[WHOLE] * len(arrays),
        out_specs=WHOLE,
        compiler_params=pltpu.CompilerParams(vmem_limit_bytes=8 * MIB),
        cost_estimate=pl.CostEstimate(flops=AHEAD, bytes_accessed=6 * rows * cols, transcendentals=rows * WIN),
    )(*arrays)


def premix_body(count, split, neg_ref, gain_ref, own_ref, *refs):
    far, near, (mix_ref, turned_ref, scaled, held) = refs[:split[0]], refs[split[0] : sum(split)], refs[sum(split) :]
    total, width = neg_ref.shape
    tall = own_ref.shape[0]
    block = 256
    gain = gain_ref[...]
    first = lax.axis_index("seq") % 2 == 0
    pieces = [own_ref]
    for k in range(1, count):
        if not near:
            pieces.append(far[k - 1])
            continue
        mine, theirs = far[(k - 1) // 2][...], near[(k - 1) // 2][...]
        even, odd = jnp.where(first, mine, theirs), jnp.where(first, theirs, mine)
        held[k - 1] = jnp.concatenate([even, odd], 0) if k == count - 1 else even if k % 2 else odd
        pieces.append(held.at[k - 1])
    for k in range(count):
        scaled[k * tall : (k + 1) * tall, :] = (pieces[k][...].astype(F32) * gain).astype(BF16)
    turn = width // (total // block)
    for n, start in enumerate(range(0, total, block)):
        part = neg_ref[start : start + block, :]
        mix_ref[start : start + block, :] = dot_last(part, scaled[...]).astype(BF16)
        cols = slice(n * turn, (n + 1) * turn)
        whole = jnp.concatenate([ref[:, cols].astype(F32) for ref in pieces], 0)
        turned_ref[cols, :] = whole.T.astype(BF16)


def premix(neg_emb, gain_row, own, far, near):
    negs, width = neg_emb.shape
    count = lax.axis_size("head")
    tall = own.shape[0]
    deep = count * tall
    return pl.pallas_call(
        functools.partial(premix_body, count, (len(far), len(near))),
        name="premix",
        out_shape=(
            jax.ShapeDtypeStruct((negs, deep), BF16),
            jax.ShapeDtypeStruct((width, deep), BF16),
        ),
        in_specs=[WHOLE] * (3 + len(far) + len(near)),
        out_specs=(WHOLE, WHOLE),
        scratch_shapes=[pltpu.VMEM((deep, width), BF16), pltpu.VMEM((count - 1, tall, width), BF16)],
        compiler_params=pltpu.CompilerParams(vmem_limit_bytes=20 * MIB),
        cost_estimate=pl.CostEstimate(flops=2 * negs * width * deep, bytes_accessed=2 * negs * width, transcendentals=0),
    )(neg_emb, gain_row, own, *far, *near)


def score_body(count, *refs):
    o_refs = refs[:count]
    mix_ref, turned_ref, id_ref, pos_ref, target_ref, stat_ref, user_ref, attn = refs[count:]
    width, rows = attn.shape
    share = user_ref.shape[0]
    negs = mix_ref.shape[0]
    block = 256
    tiles = lambda a: a.reshape(a.shape[0] // 8, 8, rows)
    heads = jnp.concatenate([ref[...] for ref in o_refs], 0)
    total = jnp.zeros((8, rows), F32)
    for start in range(0, width, block):
        part = dot_plain(turned_ref[start : start + block, :], heads)
        attn[start : start + block, :] = part
        total += jnp.sum(tiles(part * part), 0)
    scale = lax.rsqrt(jnp.sum(total, 0, keepdims=True) / width + 1e-05)
    power = scale * LOG2E
    target = target_ref[...]
    top = jnp.full((8, rows), LOW, F32)
    mass = jnp.zeros((8, rows), F32)
    for start in range(0, negs, block):
        part = dot_plain(mix_ref[start : start + block, :], heads)
        ids = id_ref[start : start + block, :]
        hit = jnp.concatenate([ids] * (rows // LANES), 1) == target
        part = tiles(jnp.where(hit, LOW, part))
        above = jnp.maximum(top, jnp.max(part, 0))
        mass = mass * jnp.exp2((top - above) * power) + jnp.sum(jnp.exp2((part - above[None]) * power[None]), 0)
        top = above
    above = jnp.max(top, 0, keepdims=True)
    mass = jnp.sum(mass * jnp.exp2((top - above) * power), 0, keepdims=True)
    here = pl.multiple_of(lax.axis_index("head") * share, share)
    user = attn[pl.ds(here, share), :] * scale
    user_ref[...] = user
    pos = jnp.sum(user * pos_ref[...], 0, keepdims=True)
    stat_ref[...] = jnp.concatenate([above * scale, mass, pos, pos], 0)


def score(heads, mix, turned, id_cols, pos_turned, target):
    count = len(heads)
    negs, deep = mix.shape
    width = turned.shape[0]
    share, rows = pos_turned.shape
    return pl.pallas_call(
        functools.partial(score_body, count),
        name="score",
        out_shape=(
            jax.ShapeDtypeStruct((4, rows), F32),
            jax.ShapeDtypeStruct((share, rows), F32),
        ),
        in_specs=[WHOLE] * (count + 5),
        out_specs=(WHOLE, WHOLE),
        scratch_shapes=[pltpu.VMEM((width, rows), F32)],
        compiler_params=pltpu.CompilerParams(vmem_limit_bytes=28 * MIB),
        cost_estimate=pl.CostEstimate(flops=2 * rows * deep * (negs + width), bytes_accessed=2 * negs * deep, transcendentals=negs * rows),
    )(*heads, mix, turned, id_cols, pos_turned, target)


def finish_body(user_ref, gain_ref, out_ref):
    out_ref[...] = (user_ref[...].T * gain_ref[...]).astype(BF16)


def finish(user, gain_here):
    share, rows = user.shape
    return pl.pallas_call(
        finish_body,
        name="finish",
        out_shape=jax.ShapeDtypeStruct((rows, share), BF16),
        in_specs=[WHOLE, WHOLE],
        out_specs=WHOLE,
        compiler_params=pltpu.CompilerParams(vmem_limit_bytes=8 * MIB),
        cost_estimate=pl.CostEstimate(flops=2 * rows * share, bytes_accessed=6 * rows * share, transcendentals=0),
    )(user, gain_here)


def on_device(
    history,
    w_query,
    w_key,
    w_value,
    w_out,
    norm_gain,
    neg_emb,
    pos_emb,
    neg_ids,
    target_ids,
    pad_mask,
):
    width = history.shape[1]
    count = lax.axis_size("head")
    query, own, edge, half = front(history, w_query, w_key, w_value, pad_mask, w_out)
    prev = from_behind(edge, "seq")
    far = fetch_in_pairs(w_out, half)
    late = attend(attend_late_body, history.shape[0] - WIN, query, own)
    mine = attend(attend_early_body, history.shape[0], query, own, prev, late)
    heads = from_all(mine, "head")
    id_cols, pos_turned, gain_here, target, gain_row = prepare(pos_emb, norm_gain, neg_ids, target_ids, width // count)
    near = swap_in_pairs(far, count)
    mix, turned = premix(neg_emb, gain_row, w_out, far, near)
    stats, user = score(heads, mix, turned, id_cols, pos_turned, target)
    all_stats = from_all(stats, "head")
    user_share = finish(user, gain_here)
    pos_logit = functools.reduce(jnp.add, [s[2] for s in all_stats])
    upper = functools.reduce(jnp.maximum, [s[0] for s in all_stats], pos_logit)
    total = functools.reduce(jnp.add, [s[1] * jnp.exp(s[0] - upper) for s in all_stats])
    loss = upper + jnp.log(total + jnp.exp(pos_logit - upper)) - pos_logit
    return (user_share, loss)


def solution(mesh):
    return jax.shard_map(
        on_device,
        mesh=mesh,
        in_specs=(
            P("seq", None),
            P(None, "head"),
            P(None, "head"),
            P(None, "head"),
            P("head", None),
            P(),
            P("head", None),
            P("seq", None),
            P("head"),
            P("seq"),
            P("seq"),
        ),
        out_specs=(P("seq", "head"), P("seq")),
        check_vma=False,
    )
```
